256 devices in a mesh: leaf: 128 (over y, x, z), panel: 2 (over core).
Axes of the slice: x: 4, y: 4, z: 8, core: 2. Of those that a mesh axis runs over, the one named last changes fastest.
Arguments:
- rhs: float32 [262144, 128], P(('leaf', 'panel')), may hold values from -6 to 6
- leaf_q: float32 [512, 512, 512], P(('leaf', 'panel')), may hold values from -0.25 to 0.25
- leaf_e: float32 [512, 384, 384], P(('leaf', 'panel')), may hold values from -0.3125 to 0.3125
- leaf_f: float32 [512, 128, 384], P(('leaf', 'panel')), may hold values from -0.15625 to 0.15625
- leaf_g: float32 [512, 384, 128], P(('leaf', 'panel')), may hold values from -0.25 to 0.25
- mid_q: float32 [256, 256, 256], P(('leaf', 'panel')), may hold values from -0.375 to 0.375
- mid_e: float32 [256, 128, 128], P(('leaf', 'panel')), may hold values from -0.5 to 0.5
- mid_f: float32 [256, 128, 128], P(('leaf', 'panel')), may hold values from -0.25 to 0.25
- mid_g: float32 [256, 128, 128], P(('leaf', 'panel')), may hold values from -0.25 to 0.25
- pair_q: float32 [128, 256, 256], P('leaf'), may hold values from -0.375 to 0.375
- pair_e: float32 [128, 128, 128], P('leaf'), may hold values from -0.5 to 0.5
- pair_f: float32 [128, 128, 128], P('leaf'), may hold values from -0.25 to 0.25
- pair_g: float32 [128, 128, 128], P('leaf'), may hold values from -0.25 to 0.25
- up_q: float32 [128, 256, 256], P('leaf'), may hold values from -0.375 to 0.375
- up_e: float32 [128, 128, 128], P('leaf'), may hold values from -0.5 to 0.5
- up_f: float32 [128, 128, 128], P('leaf'), may hold values from -0.25 to 0.25
- up_g: float32 [128, 128, 128], P('leaf'), may hold values from -0.25 to 0.25
Outputs:
- solution: float32 [262144, 128], P(('leaf', 'panel'))
The draws below stay inside these ranges and needn't reach their ends.
All inputs are finite; a program needn't handle non-finite values.
Results may differ from the reference program's by a relative error of at most 0.0003.
Values sent between devices are 32-bit elements; how exact they have to be, the bound alone decides.
A program may use at most 128 MiB of HBM per device.

```python
import jax
import jax.numpy as jnp
import numpy as np
from jax import lax

LEAF = 512
RANK = 128
COLS = 128
LEAVES_DEV = 2
LEAVES = 512
MID = 256
TREE_DEPTH = 7
LOCAL_DEPTH = 1
N_LEAF = 128
N_PANEL = 2


def shard_levels(key, dims, pieces, smallest, high):
    factor_of = 1.0
    for dim, parts in pieces:
        draws = jax.random.uniform(jax.random.fold_in(jax.random.fold_in(key, 6), dim), (parts,), jnp.float32, smallest / len(pieces), high / len(pieces))
        factor_of = factor_of * jnp.repeat(jnp.exp(draws), dims[dim] // parts).reshape((-1,) + (1,) * (len(dims) - 1 - dim))
    return factor_of


def noise(rng, dims, scale, bound, cuts=(), kind=jnp.bfloat16):
    values = scale * jax.random.normal(rng, dims, jnp.float32)
    if cuts:
        values = values * shard_levels(rng, dims, cuts, -0.22, 0.18)
    return jnp.clip(values, -bound, bound).astype(kind)


def setup_inputs(seed: int = 0) -> dict:
    key_list = jax.random.split(jax.random.key(seed), 18)
    rhs = noise(key_list[0], (LEAVES * LEAF, COLS), 1.0, 6.0, ((0, 256),), jnp.float32)
    leaf_q = noise(key_list[1], (LEAVES, LEAF, LEAF), LEAF ** -0.5, 0.25, ((0, 256),), jnp.float32)
    leaf_e = noise(key_list[2], (LEAVES, LEAF - RANK, LEAF - RANK), (LEAF - RANK) ** -0.5, 0.3125, ((0, 256),), jnp.float32)
    leaf_f = noise(key_list[3], (LEAVES, RANK, LEAF - RANK), (4 * (LEAF - RANK)) ** -0.5, 0.15625, ((0, 256),), jnp.float32)
    leaf_g = noise(key_list[4], (LEAVES, LEAF - RANK, RANK), (4 * RANK) ** -0.5, 0.25, ((0, 256),), jnp.float32)
    mid_q = noise(key_list[5], (MID, 2 * RANK, 2 * RANK), (2 * RANK) ** -0.5, 0.375, ((0, 256),), jnp.float32)
    mid_e = noise(key_list[6], (MID, RANK, RANK), RANK ** -0.5, 0.5, ((0, 256),), jnp.float32)
    mid_f = noise(key_list[7], (MID, RANK, RANK), (4 * RANK) ** -0.5, 0.25, ((0, 256),), jnp.float32)
    mid_g = noise(key_list[8], (MID, RANK, RANK), (4 * RANK) ** -0.5, 0.25, ((0, 256),), jnp.float32)
    pair_q = noise(key_list[9], (N_LEAF, 2 * RANK, 2 * RANK), (2 * RANK) ** -0.5, 0.375, ((0, 128),), jnp.float32)
    pair_e = noise(key_list[10], (N_LEAF, RANK, RANK), RANK ** -0.5, 0.5, ((0, 128),), jnp.float32)
    pair_f = noise(key_list[11], (N_LEAF, RANK, RANK), (4 * RANK) ** -0.5, 0.25, ((0, 128),), jnp.float32)
    pair_g = noise(key_list[12], (N_LEAF, RANK, RANK), (4 * RANK) ** -0.5, 0.25, ((0, 128),), jnp.float32)
    up_q = noise(key_list[13], (N_LEAF, 2 * RANK, 2 * RANK), (2 * RANK) ** -0.5, 0.375, ((0, 128),), jnp.float32)
    up_e = noise(key_list[14], (N_LEAF, RANK, RANK), RANK ** -0.5, 0.5, ((0, 128),), jnp.float32)
    up_f = noise(key_list[15], (N_LEAF, RANK, RANK), (4 * RANK) ** -0.5, 0.25, ((0, 128),), jnp.float32)
    up_g = noise(key_list[16], (N_LEAF, RANK, RANK), (4 * RANK) ** -0.5, 0.25, ((0, 128),), jnp.float32)
    return {"rhs": rhs, "leaf_q": leaf_q, "leaf_e": leaf_e, "leaf_f": leaf_f, "leaf_g": leaf_g, "mid_q": mid_q, "mid_e": mid_e, "mid_f": mid_f, "mid_g": mid_g, "pair_q": pair_q, "pair_e": pair_e, "pair_f": pair_f, "pair_g": pair_g, "up_q": up_q, "up_e": up_e, "up_f": up_f, "up_g": up_g}


highest_precision = lax.Precision.HIGHEST


def eliminate(basis, inverse_factor, coupling_block, block_in):
    eliminated_rows = inverse_factor.shape[1]
    coefficient_rows = jnp.einsum('nij,nic->njc', basis, block_in, precision=highest_precision)
    lower_block_part = jnp.einsum('gwe,gel->gwl', inverse_factor, coefficient_rows[:, :eliminated_rows], precision=highest_precision)
    reduced_system = coefficient_rows[:, eliminated_rows:] - jnp.einsum('gwe,gel->gwl', coupling_block, lower_block_part, precision=highest_precision)
    return lower_block_part, reduced_system


def substitute(basis, back_map, lower_block_part, upper_part):
    first_part = lower_block_part - jnp.einsum('gwe,gel->gwl', back_map, upper_part, precision=highest_precision)
    stacked = jnp.concatenate([first_part, upper_part], axis=1)
    return jnp.einsum('nij,njc->nic', basis, stacked, precision=highest_precision)


def reference(rhs, leaf_q, leaf_e, leaf_f, leaf_g, mid_q, mid_e, mid_f, mid_g, pair_q, pair_e, pair_f, pair_g, up_q, up_e, up_f, up_g):
    blocks = N_LEAF * N_PANEL
    columns = rhs.shape[1]
    leaf_count = rhs.shape[0] // LEAF
    leaf_lower, reduced_system = eliminate(leaf_q, leaf_e, leaf_f, rhs.reshape(leaf_count, LEAF, columns))

    def mid_slice(table, offset, pairs):
        shaped = table.reshape((blocks, LEAVES_DEV - 1) + table.shape[1:])
        return shaped[:, offset:offset + pairs].reshape((blocks * pairs,) + table.shape[1:])

    mid_saved = []
    nodes_now = LEAVES_DEV
    offset = 0
    for section_idx in range(LOCAL_DEPTH):
        pairs = nodes_now // 2
        stacked = reduced_system.reshape(blocks * pairs, 2 * RANK, columns)
        lower_block_part, reduced_system = eliminate(mid_slice(mid_q, offset, pairs), mid_slice(mid_e, offset, pairs), mid_slice(mid_f, offset, pairs), stacked)
        mid_saved.append((lower_block_part, offset, pairs))
        offset = offset + pairs
        nodes_now = pairs
    pair_lower, reduced_system = eliminate(pair_q, pair_e, pair_f, reduced_system.reshape(N_LEAF, 2 * RANK, columns))
    upper_saved = []
    for level in range(1, TREE_DEPTH + 1):
        nodes_now = N_LEAF >> level
        slots = (2 * np.arange(nodes_now) + 1) * (1 << (level - 1))
        stacked = reduced_system.reshape(nodes_now, 2 * RANK, columns)
        lower_block_part, reduced_system = eliminate(up_q[slots], up_e[slots], up_f[slots], stacked)
        upper_saved.append((lower_block_part, slots))
    upper_part = jnp.einsum('gwe,gel->gwl', up_e[0:1], reduced_system, precision=highest_precision)
    for level in range(TREE_DEPTH, 0, -1):
        lower_block_part, slots = upper_saved[level - 1]
        whole_x = substitute(up_q[slots], up_g[slots], lower_block_part, upper_part)
        upper_part = whole_x.reshape(2 * whole_x.shape[0], RANK, columns)
    whole_x = substitute(pair_q, pair_g, pair_lower, upper_part)
    upper_part = whole_x.reshape(blocks, RANK, columns)
    for lower_block_part, offset, pairs in reversed(mid_saved):
        whole_x = substitute(mid_slice(mid_q, offset, pairs), mid_slice(mid_g, offset, pairs), lower_block_part, upper_part)
        upper_part = whole_x.reshape(2 * whole_x.shape[0], RANK, columns)
    result = substitute(leaf_q, leaf_g, leaf_lower, upper_part)
    return result.reshape(leaf_count * LEAF, columns)
```

```python
import jax
import jax.numpy as jnp
from jax import lax
from jax.experimental import pallas as pl
from jax.experimental.pallas import tpu as pltpu
from jax.sharding import PartitionSpec as P

MESH = pl.DeviceIdType.MESH
F32 = jnp.float32
NAMES = "rhs lq le lf lg mq me mf mg pq pe pf pg uq ue uf ug".split()
LOADS = (
    [(n, None) for n in ("mq", "me", "mf", "mg", "pq", "pe", "pf", "pg", "uq", "ue", "uf", "ug")]
    + [("rhs", None)]
    + [(n, leaf) for leaf in (0, 1) for n in ("lq", "le", "lf", "lg")]
)


def nn(a, b):
    return lax.dot_general(
        a, b, (((1,), (0,)), ((), ())), precision=lax.Precision.HIGH, preferred_element_type=F32
    )


def nt(a, b):
    return lax.dot_general(
        a, b, (((1,), (1,)), ((), ())), precision=lax.Precision.HIGH, preferred_element_type=F32
    )


def num(flag):
    return jnp.where(flag, 1, 0)


def node_operators(q, e, f, g, mt, rt, p):
    r = e.shape[0]
    q1, q2 = q[:, :r], q[:, r:]
    tt = nt(q1, e[...])
    mt[...] = q2 - nt(tt, f[...])
    rt[...] = nt(tt, q1)
    p[...] = q2 - nn(q1, g[...])


def make_kernel(levels):
    def kernel(*refs):
        hbm = dict(zip(NAMES, refs[:17]))
        out = refs[17]
        v = dict(zip(NAMES, refs[18:35]))
        (mmt, mrt, mp, pmt, prt, pp, umt, urt, up, yl, xp, lp, bm, bp, bu, zs, ws, w0, wk, wm, wo,
         e0, load_sem, out_sem, send_sem, recv_sem) = refs[35:]
        c = lax.axis_index("leaf")
        core = lax.axis_index("panel")
        on0 = core == 0
        owner = [None] + [c % (2**k) == 2 ** (k - 1) for k in range(1, levels + 1)]
        top = 2 ** (levels - 1)

        loads = {}
        for i, (n, leaf) in enumerate(LOADS):
            src, dst = hbm[n], v[n]
            if leaf is not None:
                src, dst = src.at[leaf], dst.at[leaf]
            elif n != "rhs":
                src, dst = src.at[0], dst
            loads[n, leaf] = pltpu.make_async_copy(src, dst, load_sem.at[i])
            loads[n, leaf].start()

        def loaded(*keys):
            for n in keys:
                loads[n if isinstance(n, tuple) else (n, None)].wait()

        barrier = pltpu.get_barrier_semaphore()

        def greet(leaf, panel):
            pl.semaphore_signal(barrier, inc=1, device_id=(leaf, panel), device_id_type=MESH)

        greet(c, 1 - core)

        @pl.when(on0)
        def _():
            greet(c + 1 - 2 * (c % 2), 0)
            for k in range(1, levels + 1):
                @pl.when(owner[k])
                def _():
                    if k < levels:
                        greet(c - c % (2**(k + 1)) + 2**k, 0)
                    if k >= 2:
                        greet(c - 2 ** (k - 2), 0)
                        greet(c + 2 ** (k - 2), 0)

            @pl.when(c == 0)
            def _():
                greet(top, 0)

            @pl.when(c == top)
            def _():
                greet(0, 0)

        expected = 1
        core0 = 1
        for k in range(1, levels + 1):
            core0 = core0 + num(owner[k]) * ((1 if k < levels else 0) + (2 if k >= 2 else 0))
        core0 = core0 + num(c == 0) + num(c == top)
        expected = 1 + jnp.where(on0, core0, 0)

        def remote(src, dst, i, leaf, panel, j=None):
            j = i if j is None else j
            return pltpu.make_async_remote_copy(
                src_ref=src, dst_ref=dst, send_sem=send_sem.at[i], recv_sem=recv_sem.at[j],
                device_id=(leaf, panel), device_id_type=MESH,
            )

        loaded("mq", "me", "mf", "mg")
        node_operators(v["mq"], v["me"], v["mf"], v["mg"], mmt, mrt, mp)
        loaded("pq", "pe", "pf", "pg", "uq", "ue", "uf", "ug")

        @pl.when(on0)
        def _():
            node_operators(v["pq"], v["pe"], v["pf"], v["pg"], pmt, prt, pp)
            node_operators(v["uq"], v["ue"], v["uf"], v["ug"], umt, urt, up)

        loaded("rhs")
        r = v["ue"].shape[0]
        size = v["lq"].shape[1]
        e_rows = size - r
        for leaf in (0, 1):
            bt = v["rhs"][leaf * size : (leaf + 1) * size, :].T
            loaded(("lq", leaf))
            ct = nn(bt, v["lq"][leaf])
            loaded(("le", leaf), ("lf", leaf))
            y = nt(ct[:, :e_rows], v["le"][leaf])
            yl[leaf] = y
            bm[leaf] = ct[:, e_rows:] - nt(y, v["lf"][leaf])
        zm = nn(bm[0], mmt[:r]) + nn(bm[1], mmt[r:])

        pl.semaphore_wait(barrier, expected)
        mid_send = remote(zs, bp.at[1], 0, c, 0)
        tops = remote(v["ue"], e0, 5, top, 0)

        def leaf_parts():
            for leaf in (0, 1):
                loaded(("lg", leaf))
                q1 = v["lq"][leaf, :, :e_rows]
                xp[leaf] = nt(q1, yl[leaf])
                lp[leaf] = v["lq"][leaf, :, e_rows:] - nn(q1, v["lg"][leaf])

        @pl.when(jnp.logical_not(on0))
        def _():
            zs[...] = zm
            mid_send.start()
            leaf_parts()
            remote(wo, wm, 4, c, 1).wait_recv()
            mid_send.wait_send()

        @pl.when(on0)
        def _():
            @pl.when(c == 0)
            def _():
                tops.start()

            bp[0] = zm
            mid_send.wait_recv()
            z0 = nn(bp[0], pmt[:r]) + nn(bp[1], pmt[r:])

            z0_send = remote(zs, bu.at[0], 1, c + 1, 0, 1)

            @pl.when(c % 2 == 0)
            def _():
                zs[...] = z0
                z0_send.start()

            @pl.when(c % 2 == 1)
            def _():
                bu[1] = z0

            w_from_parent = remote(wo, wk, 2, c, 0, 3)
            w_to_even = remote(ws.at[0], w0, 3, c - 1, 0, 6)

            for k in range(1, levels + 1):
                @pl.when(owner[k])
                def _():
                    remote(zs, bu.at[0], 1, c, 0, 1).wait_recv()
                    if k >= 2:
                        remote(zs, bu.at[1], 1, c, 0, 2).wait_recv()
                    zk = nn(bu[0], umt[:r]) + nn(bu[1], umt[r:])
                    if k < levels:
                        parent = c - c % (2 ** (k + 1)) + 2**k
                        side = (c // 2**k) % 2
                        if k >= 2:
                            @pl.when(c % 2 == 0)
                            def _():
                                z0_send.wait_send()
                        zs[...] = zk
                        send = remote(zs, bu.at[side], 2, parent, 0, 1 + side)
                        send.start()
                        send.wait_send()
                    else:
                        tops.wait_recv()
                        z0_send.wait_send()
                        wk[...] = nt(zk, e0[...])

            @pl.when(c == 0)
            def _():
                z0_send.wait_send()

            leaf_parts()

            for k in range(levels, 0, -1):
                @pl.when(owner[k])
                def _():
                    if k < levels:
                        w_from_parent.wait_recv()
                    x = nn(bu[0], urt[:r]) + nn(bu[1], urt[r:]) + nt(wk[...], up[...])
                    ws[0] = x[:, :r]
                    if k >= 2:
                        ws[1] = x[:, r:]
                        left = remote(ws.at[0], wk, 3, c - 2 ** (k - 2), 0, 3)
                        right = remote(ws.at[1], wk, 4, c + 2 ** (k - 2), 0, 3)
                        left.start()
                        right.start()
                        left.wait_send()
                        right.wait_send()
                    else:
                        w_to_even.start()
                        w0[...] = x[:, r:]
                        w_to_even.wait_send()

            @pl.when(c % 2 == 0)
            def _():
                w_to_even.wait_recv()

            x = nn(bp[0], prt[:r]) + nn(bp[1], prt[r:]) + nt(w0[...], pp[...])
            wo[...] = x[:, r:]
            to_other = remote(wo, wm, 6, c, 1, 4)
            to_other.start()
            wm[...] = x[:, :r]
            to_other.wait_send()

            @pl.when(c == 0)
            def _():
                tops.wait_send()

        x = nn(bm[0], mrt[:r]) + nn(bm[1], mrt[r:]) + nt(wm[...], mp[...])
        outs = []
        for leaf in (0, 1):
            rows = slice(leaf * size, (leaf + 1) * size)
            v["rhs"][rows, :] = xp[leaf] + nt(lp[leaf], x[:, leaf * r : (leaf + 1) * r])
            outs.append(pltpu.make_async_copy(v["rhs"].at[rows], out.at[rows], out_sem.at[leaf]))
            outs[-1].start()
        for copy in outs:
            copy.wait()

    return kernel


def solution(mesh):
    levels = mesh.shape["leaf"].bit_length() - 1

    def local(*args):
        rhs, lq, le = args[0], args[1], args[2]
        r = args[14].shape[1]
        cols = rhs.shape[1]
        size, e_rows = lq.shape[1], le.shape[1]
        vm = lambda *s: pltpu.VMEM(s, F32)
        staged = [vm(*a.shape) if n[0] in "rl" else vm(*a.shape[1:]) for n, a in zip(NAMES, args)]
        operators = [vm(2 * r, r), vm(2 * r, 2 * r), vm(2 * r, r)] * 3
        scratch = staged + operators + [
            vm(2, cols, e_rows), vm(2, size, cols), vm(2, size, r),
            vm(2, cols, r), vm(2, cols, r), vm(2, cols, r),
            vm(cols, r), vm(2, cols, r), vm(cols, r), vm(cols, r), vm(cols, r), vm(cols, r),
            vm(r, r),
            pltpu.SemaphoreType.DMA((len(LOADS),)),
            pltpu.SemaphoreType.DMA((2,)),
            pltpu.SemaphoreType.DMA((8,)),
            pltpu.SemaphoreType.DMA((8,)),
        ]
        return pl.pallas_call(
            make_kernel(levels),
            out_shape=jax.ShapeDtypeStruct(rhs.shape, F32),
            in_specs=[pl.BlockSpec(memory_space=pl.ANY)] * 17,
            out_specs=pl.BlockSpec(memory_space=pl.ANY),
            scratch_shapes=scratch,
            compiler_params=pltpu.CompilerParams(
                collective_id=0, has_side_effects=True, vmem_limit_bytes=48 << 20
            ),
        )(*args)

    both, one = P(("leaf", "panel"), None, None), P("leaf", None, None)
    return jax.shard_map(
        local,
        mesh=mesh,
        in_specs=(P(("leaf", "panel"), None),) + (both,) * 8 + (one,) * 8,
        out_specs=P(("leaf", "panel"), None),
        check_vma=False,
    )
```

```python
import functools

import jax
import jax.numpy as jnp
from jax import lax
from jax.experimental import pallas as pl
from jax.experimental.pallas import tpu as pltpu
from jax.sharding import PartitionSpec as P

MESH = pl.DeviceIdType.MESH
F32 = jnp.float32
NAMES = (
    ("rhs",)
    + ("lq", "le", "lf", "lg")
    + ("mq", "me", "mf", "mg")
    + ("pq", "pe", "pf", "pg")
    + ("uq", "ue", "uf", "ug")
)
LOADS = (
    [(n, None) for n in NAMES[13:] + NAMES[9:13] + NAMES[5:9]]
    + [("rhs", None)]
    + [(n, leaf) for leaf in (0, 1) for n in NAMES[1:4]]
    + [("lg", 0), ("lg", 1)]
)
RING, LINE = 8, 4


def nn(a, b):
    return lax.dot_general(
        a, b, (((1,), (0,)), ((), ())), precision=lax.Precision.HIGH, preferred_element_type=F32
    )


def nt(a, b):
    return lax.dot_general(
        a, b, (((1,), (1,)), ((), ())), precision=lax.Precision.HIGH, preferred_element_type=F32
    )


def pairs(b0, b1, m):
    r = b0.shape[1]
    return nn(b0, m[:r]) + nn(b1, m[r:])


def node_operators(q, e, f, g, mt, rt, p):
    r = e.shape[0]
    q1, q2 = q[:, :r], q[:, r:]
    tt = nt(q1, e[...])
    mt[...] = q2 - nt(tt, f[...])
    for s in (0, 1):
        rows = slice(s * r, (s + 1) * r)
        rt[s] = nt(tt, q1[rows])
        p[s] = q2[rows] - nn(q1[rows], g[...])


def scratch_of(r, cols, size, e_rows):
    block, half = (cols, r), (2 * r, r)
    ops = {}
    for n in ("m", "p", "u"):
        ops |= {n + "mt": half, n + "rt": (2, *half), n + "p": (2, r, r)}
    return ops | {
        "yl": (2, cols, e_rows), "xp": (2, size, cols), "lp": (2, size, r),
        "bm": (2, *block), "bp": (2, *block), "zm": block, "wm": block, "wo": block,
        "um": (2, *block), "upair": (2, *block), "z0": block, "sib": block, "u1": block,
        "w1": block, "rt1": half, "p1": (r, r),
        "zg": (RING, *block), "z1": (4, *block), "z2": (2, *block), "w1s": (4, *block),
        "m1": (4, *half), "m2": (2, *half), "m3": half,
        "rt2": (2, 2, *half), "p2": (2, 2, r, r), "rt3": (2, *half), "p3": (2, r, r),
        "uz2": (2, 2, *block), "uz3": (2, *block), "z4": (2, *block),
        "x3": (LINE, *block), "y5": (LINE, *block), "u4": block, "u5": block,
        "m4": (2, *half), "m5": half, "rt4": half, "p4": (r, r), "rt5": half, "p5": (r, r),
        "tt": (4 * r, r),
        "e0": (r, r), "my": (2, *half), "rt6": half, "p6": (r, r), "k7": half,
        "k7s": (2, *half), "tts": (4 * r, r),
    }


SLOTS = (
    [("bp", i) for i in (0, 1)]
    + [("zg", i) for i in range(RING)]
    + [(n, i) for n in ("m1", "x3", "y5") for i in range(LINE)]
    + [(n, i) for n in ("m2", "rt2", "p2", "m4", "my") for i in (0, 1)]
    + [(n, 0) for n in ("wm", "sib", "w1", "rt1", "p1", "m3", "rt3", "p3", "m5")]
    + [(n, 0) for n in ("rt4", "p4", "rt5", "p5", "tt", "e0", "rt6", "p6", "k7")]
)
SENDS = 72


def kernel(names, *refs):
    n_in = len(NAMES)
    hbm, out = dict(zip(NAMES, refs[:n_in])), refs[n_in]
    refs = refs[n_in + 1 :]
    v, refs = dict(zip(NAMES, refs[:n_in])), refs[n_in:]
    t, refs = dict(zip(names, refs)), refs[len(names) :]
    load_sem, out_sem, send_sem, recv_sem = refs
    c, core = lax.axis_index("leaf"), lax.axis_index("panel")
    z, x, y = c % RING, (c // RING) % LINE, c // (RING * LINE)
    both = jnp.logical_and
    on0, on1 = core == 0, core == 1
    head0, head1 = both(on0, z == 0), both(on1, z == 0)
    column = both(head1, x == 0)
    inner = both(on0, z > 0)
    ring = c - z
    at_x = lambda q: c - RING * x + RING * q
    at_y = lambda q: c - RING * LINE * y + RING * LINE * q
    others = lambda i: [(i + d) % LINE for d in (1, 3, 2)]

    loads = {}
    for i, (n, leaf) in enumerate(LOADS):
        src, dst = hbm[n], v[n]
        if leaf is not None:
            src, dst = src.at[leaf], dst.at[leaf]
        elif n != "rhs":
            src = src.at[0]
        loads[n, leaf] = pltpu.make_async_copy(src, dst, load_sem.at[i])
        if n[0] in "up":
            pl.when(on1 if n[0] == "u" else on0)(loads[n, leaf].start)
        else:
            loads[n, leaf].start()

    def loaded(*keys):
        for n in keys:
            loads[n if isinstance(n, tuple) else (n, None)].wait()

    barrier = pltpu.get_barrier_semaphore()
    expected = []

    def greet(when, *devices):
        @pl.when(when)
        def _():
            for device in devices:
                pl.semaphore_signal(barrier, inc=1, device_id=device, device_id_type=MESH)

        expected.append(jnp.where(when, len(devices), 0))

    pl.semaphore_signal(barrier, inc=1, device_id=(c, 1 - core), device_id_type=MESH)
    greet(on0, (c + 1 - 2 * (z % 2), 0))
    greet(z > 0, (ring, 0))
    greet(both(on1, z % 2 == 1), (c - 1, 0))
    greet(both(on0, z % 2 == 0), (c + 1, 1))
    greet(head0, *((c + d, panel) for d in range(1, RING) for panel in (0, 1)))
    greet(head0, *((at_x(q), panel) for q in others(x) for panel in (0, 1)))
    greet(head0, *((at_y(q), 0) for q in others(y)))
    greet(head1, *((at_x(q), 0) for q in others(x)))
    greet(column, *((at_y(q), 1) for q in others(y)))

    pending = []

    def slot(name, index):
        ref = t[name] if name in ALONE else t[name].at[index]
        return ref, recv_sem.at[SLOTS.index((name, 0)) + index]

    def copy_to(sem, src, device, name, index=0):
        dst, arrival = slot(name, index)
        return pltpu.make_async_remote_copy(
            src_ref=src, dst_ref=dst, send_sem=send_sem.at[sem], recv_sem=arrival,
            device_id=device, device_id_type=MESH,
        )

    used = [0]

    def send(when, *messages):
        copies = []
        for message in messages:
            copies.append(copy_to(used[0], *message))
            used[0] += 1
        pending.append((when, copies))

        @pl.when(when)
        def _():
            for copy in copies:
                copy.start()

    def sent():
        for when, copies in pending:
            @pl.when(when)
            def _():
                for copy in copies:
                    copy.wait_send()

        pending.clear()

    def arrived(name, index=0):
        copy_to(0, slot(name, index)[0], (c, 1 - core), name, index).wait_recv()

    r = v["ue"].shape[0]
    size = v["lq"].shape[1]
    e_rows = size - r

    def operators(n):
        loaded(*(n + k for k in "qefg"))
        node_operators(*(v[n + k] for k in "qefg"), t[n + "mt"], t[n + "rt"], t[n + "p"])

    umt, urt, up = t["umt"], t["urt"], t["up"]
    pl.when(on1)(lambda: operators("u"))
    pl.semaphore_wait(barrier, 1 + sum(expected[1:], expected[0]))
    send(both(column, y == 0), (v["ue"], (at_y(2), 1), "e0"))
    send(
        both(on1, z % 2 == 1),
        (umt, (ring, 0), "m1", z // 2),
        *((urt.at[s], (c - 1 + s, 0), "rt1") for s in (0, 1)),
        *((up.at[s], (c - 1 + s, 0), "p1") for s in (0, 1)),
    )
    send(
        both(on1, z % 4 == 2),
        (umt, (ring, 0), "m2", z // 4),
        (urt, (ring, 0), "rt2", z // 4),
        (up, (ring, 0), "p2", z // 4),
    )
    send(
        both(on1, z == 4),
        (umt, (ring, 0), "m3"),
        (urt, (ring, 0), "rt3"),
        (up, (ring, 0), "p3"),
    )
    send(
        both(head1, x % 2 == 1),
        *((umt, (at_x(q), 0), "m4", x // 2) for q in others(x) + [x]),
        *((urt.at[s], (at_x(x - 1 + s), 0), "rt4") for s in (0, 1)),
        *((up.at[s], (at_x(x - 1 + s), 0), "p4") for s in (0, 1)),
    )
    send(
        both(head1, x == 2),
        *((umt, (at_x(q), 0), "m5") for q in others(x) + [x]),
        *((urt.at[q // 2], (at_x(q), 0), "rt5") for q in range(LINE)),
        *((up.at[q // 2], (at_x(q), 0), "p5") for q in range(LINE)),
    )
    send(
        both(column, y % 2 == 1),
        *((umt, (at_y(q), 1), "my", y // 2) for q in others(y)),
        (urt.at[0], (at_y(y - 1), 1), "rt6"),
        (up.at[0], (at_y(y - 1), 1), "p6"),
    )

    operators("m")
    pl.when(on0)(lambda: operators("p"))

    loaded("rhs")
    bm, yl, bp = t["bm"], t["yl"], t["bp"]
    for leaf in (0, 1):
        bt = v["rhs"][leaf * size : (leaf + 1) * size, :].T
        loaded(("lq", leaf))
        ct = nn(bt, v["lq"][leaf])
        loaded(("le", leaf), ("lf", leaf))
        yt = nt(ct[:, :e_rows], v["le"][leaf])
        yl[leaf] = yt
        bm[leaf] = ct[:, e_rows:] - nt(yt, v["lf"][leaf])
    t["zm"][...] = pairs(bm[0], bm[1], t["mmt"])
    send(on1, (t["zm"], (c, 0), "bp", 1))

    @pl.when(both(column, y == 2))
    def _():
        arrived("e0")
        w7 = nt(umt[...], t["e0"][...])
        for s in (0, 1):
            t["k7s"][s] = urt[s] + nt(w7, up[s])
        t["k7"][...] = t["k7s"][1]

    send(
        both(column, y == 2),
        *((t["k7s"].at[q // 2], (at_y(q), 1), "k7") for q in (1, 3, 0)),
    )
    for a in (0, 1):
        @pl.when(both(column, y == 2 * a + 1))
        def _():
            t["my"][a] = umt[...]
            t["rt6"][...] = urt[1]
            t["p6"][...] = up[1]

        pl.when(both(column, y != 2 * a + 1))(lambda: arrived("my", a))

    @pl.when(both(column, y % 2 == 0))
    def _():
        arrived("rt6")
        arrived("p6")

    pl.when(both(column, y != 2))(lambda: arrived("k7"))

    @pl.when(column)
    def _():
        p6 = t["p6"][...]
        for a in (0, 1):
            rows = slice(2 * a * r, 2 * (a + 1) * r)
            own = jnp.where(y // 2 == a, t["rt6"][...], 0.0)
            t["tts"][rows] = nt(nn(t["my"][a], t["k7"][a * r : (a + 1) * r]), p6) + own

    send(column, *((t["tts"], (at_x(q), 0), "tt") for q in (1, 3, 2, 0)))

    zg, x3, y5 = t["zg"], t["x3"], t["y5"]

    @pl.when(on0)
    def _():
        bp[0] = t["zm"][...]
        arrived("bp", 1)
        z0 = pairs(bp[0], bp[1], t["pmt"])
        t["z0"][...] = z0
        zg[0] = z0

    send(inner, (t["z0"], (ring, 0), "zg", z))
    send(on0, (t["z0"], (c + 1 - 2 * (z % 2), 0), "sib"))

    for leaf in (0, 1):
        loaded(("lg", leaf))
        q1 = v["lq"][leaf, :, :e_rows]
        t["xp"][leaf] = nt(q1, yl[leaf])
        t["lp"][leaf] = v["lq"][leaf, :, e_rows:] - nn(q1, v["lg"][leaf])
        t["um"][leaf] = pairs(bm[0], bm[1], t["mrt"].at[leaf])

    @pl.when(on0)
    def _():
        for s in (0, 1):
            t["upair"][s] = pairs(bp[0], bp[1], t["prt"].at[s])

    def level_one():
        arrived("rt1")
        arrived("p1")
        arrived("sib")
        first = jnp.where(z % 2 == 0, t["z0"][...], t["sib"][...])
        second = jnp.where(z % 2 == 0, t["sib"][...], t["z0"][...])
        t["u1"][...] = pairs(first, second, t["rt1"])

    @pl.when(inner)
    def _():
        level_one()

    @pl.when(head0)
    def _():
        for j in (0, 3, 1, 2):
            arrived("m1", j)
            for i in (2 * j, 2 * j + 1):
                if i:
                    arrived("zg", i)
            t["z1"][j] = pairs(zg[2 * j], zg[2 * j + 1], t["m1"].at[j])
        for j in (0, 1):
            arrived("m2", j)
            t["z2"][j] = pairs(t["z1"][2 * j], t["z1"][2 * j + 1], t["m2"].at[j])
        arrived("m3")
        x3[x] = pairs(t["z2"][0], t["z2"][1], t["m3"])

    send(head0, *((x3.at[x], (at_x(q), 0), "x3", x) for q in others(x)))

    @pl.when(head0)
    def _():
        for a in (0, 1):
            arrived("m4", a)
        arrived("m5")
        for q in others(x):
            arrived("x3", q)
        for a in (0, 1):
            t["z4"][a] = pairs(x3[2 * a], x3[2 * a + 1], t["m4"].at[a])
        y5[y] = pairs(t["z4"][0], t["z4"][1], t["m5"])

    send(head0, *((y5.at[y], (at_y(q), 0), "y5", y) for q in others(y)))

    @pl.when(head0)
    def _():
        for n in ("rt5", "p5", "rt4", "p4", "rt3", "p3"):
            arrived(n)
        t["u5"][...] = pairs(t["z4"][0], t["z4"][1], t["rt5"])
        t["u4"][...] = pairs(x3[2 * (x // 2)], x3[2 * (x // 2) + 1], t["rt4"])
        for s in (0, 1):
            t["uz3"][s] = pairs(t["z2"][0], t["z2"][1], t["rt3"].at[s])
        for i in (0, 1):
            arrived("rt2", i)
            arrived("p2", i)
            for s in (0, 1):
                t["uz2"][i, s] = pairs(t["z1"][2 * i], t["z1"][2 * i + 1], t["rt2"].at[i, s])
        level_one()
        arrived("tt")
        for q in others(y):
            arrived("y5", q)
        w5 = sum(nn(y5[q], t["tt"][q * r : (q + 1) * r]) for q in range(LINE))
        w4 = t["u5"][...] + nt(w5, t["p5"][...])
        w3 = t["u4"][...] + nt(w4, t["p4"][...])
        for i in (0, 1):
            w2 = t["uz3"][i] + nt(w3, t["p3"][i])
            for s in (0, 1):
                t["w1s"][2 * i + s] = t["uz2"][i, s] + nt(w2, t["p2"][i, s])
        t["w1"][...] = t["w1s"][0]

    send(
        head0,
        *((t["w1s"].at[i // 2], (c + i, 0), "w1") for i in (4, 5, 3, 6, 2, 7, 1)),
    )
    late = pending.pop()
    sent()

    @pl.when(on0)
    def _():
        pl.when(z > 0)(lambda: arrived("w1"))
        w0 = t["u1"][...] + nt(t["w1"][...], t["p1"][...])
        t["wo"][...] = t["upair"][1] + nt(w0, t["pp"][1])
        t["wm"][...] = t["upair"][0] + nt(w0, t["pp"][0])

    send(on0, (t["wo"], (c, 1), "wm"))
    pl.when(on1)(lambda: arrived("wm"))
    wm = t["wm"][...]
    outs = []
    for leaf in (0, 1):
        w = t["um"][leaf] + nt(wm, t["mp"][leaf])
        rows = slice(leaf * size, (leaf + 1) * size)
        v["rhs"][rows, :] = t["xp"][leaf] + nt(t["lp"][leaf], w)
        outs.append(pltpu.make_async_copy(v["rhs"].at[rows], out.at[rows], out_sem.at[leaf]))
        outs[-1].start()
    for copy in outs:
        copy.wait()
    pending.append(late)
    sent()


ALONE = frozenset(n for n, _ in SLOTS if (n, 1) not in SLOTS)


def solution(mesh):
    def local(*args):
        rhs, lq, le = args[:3]
        r, cols = args[14].shape[1], rhs.shape[1]
        vm = lambda s: pltpu.VMEM(s, F32)
        staged = [vm(a.shape if n[0] in "rl" else a.shape[1:]) for n, a in zip(NAMES, args)]
        more = scratch_of(r, cols, lq.shape[1], le.shape[1])
        scratch = staged + [vm(s) for s in more.values()]
        scratch += [pltpu.SemaphoreType.DMA((n,)) for n in (len(LOADS), 2, SENDS, len(SLOTS))]
        return pl.pallas_call(
            functools.partial(kernel, tuple(more)),
            out_shape=jax.ShapeDtypeStruct(rhs.shape, F32),
            in_specs=[pl.BlockSpec(memory_space=pl.ANY)] * len(NAMES),
            out_specs=pl.BlockSpec(memory_space=pl.ANY),
            scratch_shapes=scratch,
            compiler_params=pltpu.CompilerParams(
                collective_id=0, has_side_effects=True, vmem_limit_bytes=60 * 1024 * 1024
            ),
        )(*args)

    leaves, chips = P(("leaf", "panel"), None, None), P("leaf", None, None)
    return jax.shard_map(
        local,
        mesh=mesh,
        in_specs=(P(("leaf", "panel"), None),) + (leaves,) * 8 + (chips,) * 8,
        out_specs=P(("leaf", "panel"), None),
        check_vma=False,
    )
```

```python
import functools

import jax
import jax.numpy as jnp
from jax import lax
from jax.experimental import pallas as pl
from jax.experimental.pallas import tpu as pltpu
from jax.sharding import PartitionSpec as P

MESH = pl.DeviceIdType.MESH
F32 = jnp.float32
NAMES = (
    ("rhs",)
    + ("lq", "le", "lf", "lg")
    + ("mq", "me", "mf", "mg")
    + ("pq", "pe", "pf", "pg")
    + ("uq", "ue", "uf", "ug")
)
LOADS = (
    [(n, None) for n in NAMES[13:] + NAMES[9:13] + NAMES[5:9]]
    + [("rhs", None)]
    + [(n, leaf) for leaf in (0, 1) for n in NAMES[1:4]]
    + [("lg", 0), ("lg", 1)]
)
RING, LINE = 8, 4


def nn(a, b):
    return lax.dot_general(
        a, b, (((1,), (0,)), ((), ())), precision=lax.Precision.HIGH, preferred_element_type=F32
    )


def nt(a, b):
    return lax.dot_general(
        a, b, (((1,), (1,)), ((), ())), precision=lax.Precision.HIGH, preferred_element_type=F32
    )


def pairs(b0, b1, m):
    r = b0.shape[1]
    return nn(b0, m[:r]) + nn(b1, m[r:])


def node_operators(q, e, f, g, mt, rt, p):
    r = e.shape[0]
    q1, q2 = q[:, :r], q[:, r:]
    tt = nt(q1, e[...])
    mt[...] = q2 - nt(tt, f[...])
    for s in (0, 1):
        rows = slice(s * r, (s + 1) * r)
        rt[s] = nt(tt, q1[rows])
        p[s] = q2[rows] - nn(q1[rows], g[...])


def scratch_of(r, cols, size, e_rows):
    block, half = (cols, r), (2 * r, r)
    ops = {}
    for n in ("m", "p", "u"):
        ops |= {n + "mt": half, n + "rt": (2, *half), n + "p": (2, r, r)}
    return ops | {
        "yl": (2, cols, e_rows), "xp": (2, size, cols), "lp": (2, size, r),
        "bm": (2, *block), "bp": (2, *block), "zm": block, "wm": block, "wo": block,
        "um": (2, *block), "upair": (2, *block), "z0": block, "sib": block, "u1": block,
        "w1": block, "rt1": half, "p1": (r, r),
        "zg": (RING, *block), "z1": (4, *block), "z2": (2, *block), "w1s": (4, *block),
        "m1": (4, *half), "m2": (2, *half), "m3": half,
        "rt2": (2, 2, *half), "p2": (2, 2, r, r), "rt3": (2, *half), "p3": (2, r, r),
        "uz2": (2, 2, *block), "uz3": (2, *block), "z4": (2, *block),
        "x3": (LINE, *block), "y5": (LINE, *block), "u4": block, "u5": block,
        "m4": (2, *half), "m5": half, "rt4": half, "p4": (r, r), "rt5": half, "p5": (r, r),
        "tt": (4 * r, r),
        "e0": (r, r), "my": (2, *half), "rt6": half, "p6": (r, r), "k7": half,
        "k7s": (2, *half), "tts": (4 * r, r),
    }


SLOTS = (
    [("bp", i) for i in (0, 1)]
    + [("zg", i) for i in range(RING)]
    + [(n, i) for n in ("m1", "x3", "y5") for i in range(LINE)]
    + [(n, i) for n in ("m2", "rt2", "p2", "m4", "my") for i in (0, 1)]
    + [(n, 0) for n in ("wm", "sib", "w1", "rt1", "p1", "m3", "rt3", "p3", "m5")]
    + [(n, 0) for n in ("rt4", "p4", "rt5", "p5", "tt", "e0", "rt6", "p6", "k7")]
)
SENDS = 72


def kernel(names, *refs):
    n_in = len(NAMES)
    hbm, out = dict(zip(NAMES, refs[:n_in])), refs[n_in]
    refs = refs[n_in + 1 :]
    v, refs = dict(zip(NAMES, refs[:n_in])), refs[n_in:]
    t, refs = dict(zip(names, refs)), refs[len(names) :]
    load_sem, out_sem, send_sem, recv_sem, go = refs
    c, core = lax.axis_index("leaf"), lax.axis_index("panel")
    z, x, y = c % RING, (c // RING) % LINE, c // (RING * LINE)
    both = jnp.logical_and
    on0, on1 = core == 0, core == 1
    head0, head1 = both(on0, z == 0), both(on1, z == 0)
    column = both(head1, x == 0)
    inner = both(on0, z > 0)
    ring = c - z
    at_x = lambda q: c - RING * x + RING * q
    at_y = lambda q: c - RING * LINE * y + RING * LINE * q
    others = lambda i: [(i + d) % LINE for d in (1, 3, 2)]

    barrier = pltpu.get_barrier_semaphore()
    expected = []

    def greet(when, *devices):
        @pl.when(when)
        def _():
            for device in devices:
                pl.semaphore_signal(barrier, inc=1, device_id=device, device_id_type=MESH)

        expected.append(jnp.where(when, len(devices), 0))

    pl.semaphore_signal(barrier, inc=1, device_id=(c, 1 - core), device_id_type=MESH)
    greet(on0, (c + 1 - 2 * (z % 2), 0))
    greet(z > 0, (ring, 0))
    greet(both(on1, z % 2 == 1), (c - 1, 0))
    greet(both(on0, z % 2 == 0), (c + 1, 1))
    greet(head0, *((c + d, panel) for d in range(1, RING) for panel in (0, 1)))
    greet(head0, *((at_x(q), panel) for q in others(x) for panel in (0, 1)))
    greet(head0, *((at_y(q), 0) for q in others(y)))
    greet(head1, *((at_x(q), 0) for q in others(x)))
    greet(column, *((at_y(q), 1) for q in others(y)))

    loads = {}
    for i, (n, leaf) in enumerate(LOADS):
        src, dst = hbm[n], v[n]
        if leaf is not None:
            src, dst = src.at[leaf], dst.at[leaf]
        elif n != "rhs":
            src = src.at[0]
        loads[n, leaf] = pltpu.make_async_copy(src, dst, load_sem.at[i])
        if n[0] in "up":
            pl.when(on1 if n[0] == "u" else on0)(loads[n, leaf].start)
        else:
            loads[n, leaf].start()

    def loaded(*keys):
        for n in keys:
            loads[n if isinstance(n, tuple) else (n, None)].wait()

    pending = []

    def slot(name, index):
        ref = t[name] if name in ALONE else t[name].at[index]
        return ref, recv_sem.at[SLOTS.index((name, 0)) + index]

    def copy_to(sem, src, device, name, index=0):
        dst, arrival = slot(name, index)
        return pltpu.make_async_remote_copy(
            src_ref=src, dst_ref=dst, send_sem=send_sem.at[sem], recv_sem=arrival,
            device_id=device, device_id_type=MESH,
        )

    used = [0]

    def send(when, *messages):
        copies = []
        for message in messages:
            copies.append(copy_to(used[0], *message))
            used[0] += 1
        pending.append((when, copies))

        @pl.when(when)
        def _():
            for copy in copies:
                copy.start()

    def sent():
        for when, copies in pending:
            @pl.when(when)
            def _():
                for copy in copies:
                    copy.wait_send()

        pending.clear()

    def arrived(name, index=0):
        copy_to(0, slot(name, index)[0], (c, 1 - core), name, index).wait_recv()

    r = v["ue"].shape[0]
    size = v["lq"].shape[1]
    e_rows = size - r

    def operators(n):
        loaded(*(n + k for k in "qefg"))
        node_operators(*(v[n + k] for k in "qefg"), t[n + "mt"], t[n + "rt"], t[n + "p"])

    umt, urt, up = t["umt"], t["urt"], t["up"]
    pl.when(on1)(lambda: operators("u"))
    pl.semaphore_wait(barrier, 1 + sum(expected[1:], expected[0]))
    send(both(column, y == 0), (v["ue"], (at_y(2), 1), "e0"))
    send(
        both(on1, z % 2 == 1),
        (umt, (ring, 0), "m1", z // 2),
        *((urt.at[s], (c - 1 + s, 0), "rt1") for s in (0, 1)),
        *((up.at[s], (c - 1 + s, 0), "p1") for s in (0, 1)),
    )
    send(both(on1, z % 4 == 2), (umt, (ring, 0), "m2", z // 4))
    send(both(on1, z == 4), (umt, (ring, 0), "m3"))
    send(
        both(head1, x % 2 == 1),
        *((umt, (at_x(q), 0), "m4", x // 2) for q in others(x) + [x]),
        *((urt.at[s], (at_x(x - 1 + s), 0), "rt4") for s in (0, 1)),
        *((up.at[s], (at_x(x - 1 + s), 0), "p4") for s in (0, 1)),
    )
    send(
        both(head1, x == 2),
        *((umt, (at_x(q), 0), "m5") for q in others(x) + [x]),
        *((urt.at[q // 2], (at_x(q), 0), "rt5") for q in range(LINE)),
        *((up.at[q // 2], (at_x(q), 0), "p5") for q in range(LINE)),
    )
    send(
        both(column, y % 2 == 1),
        *((umt, (at_y(q), 1), "my", y // 2) for q in others(y)),
        (urt.at[0], (at_y(y - 1), 1), "rt6"),
        (up.at[0], (at_y(y - 1), 1), "p6"),
    )

    operators("m")
    pl.when(on0)(lambda: operators("p"))

    loaded("rhs")
    bm, yl, bp = t["bm"], t["yl"], t["bp"]
    for leaf in (0, 1):
        bt = v["rhs"][leaf * size : (leaf + 1) * size, :].T
        loaded(("lq", leaf))
        ct = nn(bt, v["lq"][leaf])
        loaded(("le", leaf), ("lf", leaf))
        yt = nt(ct[:, :e_rows], v["le"][leaf])
        yl[leaf] = yt
        bm[leaf] = ct[:, e_rows:] - nt(yt, v["lf"][leaf])
    t["zm"][...] = pairs(bm[0], bm[1], t["mmt"])
    send(on1, (t["zm"], (c, 0), "bp", 1))

    @pl.when(both(column, y == 2))
    def _():
        arrived("e0")
        w7 = nt(umt[...], t["e0"][...])
        for s in (0, 1):
            t["k7s"][s] = urt[s] + nt(w7, up[s])
        t["k7"][...] = t["k7s"][1]

    send(
        both(column, y == 2),
        *((t["k7s"].at[q // 2], (at_y(q), 1), "k7") for q in (1, 3, 0)),
    )
    for a in (0, 1):
        @pl.when(both(column, y == 2 * a + 1))
        def _():
            t["my"][a] = umt[...]
            t["rt6"][...] = urt[1]
            t["p6"][...] = up[1]

        pl.when(both(column, y != 2 * a + 1))(lambda: arrived("my", a))

    @pl.when(both(column, y % 2 == 0))
    def _():
        arrived("rt6")
        arrived("p6")

    pl.when(both(column, y != 2))(lambda: arrived("k7"))

    @pl.when(column)
    def _():
        p6 = t["p6"][...]
        for a in (0, 1):
            rows = slice(2 * a * r, 2 * (a + 1) * r)
            own = jnp.where(y // 2 == a, t["rt6"][...], 0.0)
            t["tts"][rows] = nt(nn(t["my"][a], t["k7"][a * r : (a + 1) * r]), p6) + own

    send(column, *((t["tts"], (at_x(q), 0), "tt") for q in (1, 3, 2, 0)))

    zg, x3, y5 = t["zg"], t["x3"], t["y5"]

    @pl.when(on0)
    def _():
        bp[0] = t["zm"][...]
        arrived("bp", 1)
        z0 = pairs(bp[0], bp[1], t["pmt"])
        t["z0"][...] = z0
        zg[0] = z0

    send(inner, (t["z0"], (ring, 0), "zg", z))
    send(on0, (t["z0"], (c + 1 - 2 * (z % 2), 0), "sib"))

    for leaf in (0, 1):
        loaded(("lg", leaf))
        q1 = v["lq"][leaf, :, :e_rows]
        t["xp"][leaf] = nt(q1, yl[leaf])
        t["lp"][leaf] = v["lq"][leaf, :, e_rows:] - nn(q1, v["lg"][leaf])
        t["um"][leaf] = pairs(bm[0], bm[1], t["mrt"].at[leaf])

    pl.when(both(on1, both(z > 0, z % 2 == 0)))(lambda: pl.semaphore_wait(go, 1))
    send(both(on1, z == 4), (urt, (ring, 0), "rt3"), (up, (ring, 0), "p3"))
    send(
        both(on1, z % 4 == 2),
        (urt, (ring, 0), "rt2", z // 4),
        (up, (ring, 0), "p2", z // 4),
    )

    @pl.when(on0)
    def _():
        for s in (0, 1):
            t["upair"][s] = pairs(bp[0], bp[1], t["prt"].at[s])

    def level_one():
        arrived("rt1")
        arrived("p1")
        arrived("sib")
        first = jnp.where(z % 2 == 0, t["z0"][...], t["sib"][...])
        second = jnp.where(z % 2 == 0, t["sib"][...], t["z0"][...])
        t["u1"][...] = pairs(first, second, t["rt1"])

    @pl.when(inner)
    def _():
        level_one()

    @pl.when(head0)
    def _():
        for j in (0, 3, 1, 2):
            arrived("m1", j)
            for i in (2 * j, 2 * j + 1):
                if i:
                    arrived("zg", i)
            if j == 0:
                for i in (4, 2, 6):
                    pl.semaphore_signal(go, inc=1, device_id=(c + i, 1), device_id_type=MESH)
            t["z1"][j] = pairs(zg[2 * j], zg[2 * j + 1], t["m1"].at[j])
        for j in (0, 1):
            arrived("m2", j)
            t["z2"][j] = pairs(t["z1"][2 * j], t["z1"][2 * j + 1], t["m2"].at[j])
        arrived("m3")
        x3[x] = pairs(t["z2"][0], t["z2"][1], t["m3"])

    send(head0, *((x3.at[x], (at_x(q), 0), "x3", x) for q in others(x)))

    @pl.when(head0)
    def _():
        for a in (0, 1):
            arrived("m4", a)
        arrived("m5")
        for q in others(x):
            arrived("x3", q)
        for a in (0, 1):
            t["z4"][a] = pairs(x3[2 * a], x3[2 * a + 1], t["m4"].at[a])
        y5[y] = pairs(t["z4"][0], t["z4"][1], t["m5"])

    send(head0, *((y5.at[y], (at_y(q), 0), "y5", y) for q in others(y)))

    @pl.when(head0)
    def _():
        for n in ("rt5", "p5", "rt4", "p4", "rt3", "p3"):
            arrived(n)
        t["u5"][...] = pairs(t["z4"][0], t["z4"][1], t["rt5"])
        t["u4"][...] = pairs(x3[2 * (x // 2)], x3[2 * (x // 2) + 1], t["rt4"])
        for s in (0, 1):
            t["uz3"][s] = pairs(t["z2"][0], t["z2"][1], t["rt3"].at[s])
        for i in (0, 1):
            arrived("rt2", i)
            arrived("p2", i)
            for s in (0, 1):
                t["uz2"][i, s] = pairs(t["z1"][2 * i], t["z1"][2 * i + 1], t["rt2"].at[i, s])
        level_one()
        arrived("tt")
        for q in others(y):
            arrived("y5", q)
        w5 = sum(nn(y5[q], t["tt"][q * r : (q + 1) * r]) for q in range(LINE))
        w4 = t["u5"][...] + nt(w5, t["p5"][...])
        w3 = t["u4"][...] + nt(w4, t["p4"][...])
        for i in (0, 1):
            w2 = t["uz3"][i] + nt(w3, t["p3"][i])
            for s in (0, 1):
                t["w1s"][2 * i + s] = t["uz2"][i, s] + nt(w2, t["p2"][i, s])
        t["w1"][...] = t["w1s"][0]

    send(
        head0,
        *((t["w1s"].at[i // 2], (c + i, 0), "w1") for i in (4, 5, 3, 6, 2, 7, 1)),
    )
    late = pending.pop()
    sent()

    @pl.when(on0)
    def _():
        pl.when(z > 0)(lambda: arrived("w1"))
        w0 = t["u1"][...] + nt(t["w1"][...], t["p1"][...])
        t["wo"][...] = t["upair"][1] + nt(w0, t["pp"][1])
        t["wm"][...] = t["upair"][0] + nt(w0, t["pp"][0])

    send(on0, (t["wo"], (c, 1), "wm"))
    pl.when(on1)(lambda: arrived("wm"))
    wm = t["wm"][...]
    outs = []
    for leaf in (0, 1):
        w = t["um"][leaf] + nt(wm, t["mp"][leaf])
        rows = slice(leaf * size, (leaf + 1) * size)
        v["rhs"][rows, :] = t["xp"][leaf] + nt(t["lp"][leaf], w)
        outs.append(pltpu.make_async_copy(v["rhs"].at[rows], out.at[rows], out_sem.at[leaf]))
        outs[-1].start()
    for copy in outs:
        copy.wait()
    pending.append(late)
    sent()


ALONE = frozenset(n for n, _ in SLOTS if (n, 1) not in SLOTS)


def solution(mesh):
    def local(*args):
        rhs, lq, le = args[:3]
        r, cols = args[14].shape[1], rhs.shape[1]
        vm = lambda s: pltpu.VMEM(s, F32)
        staged = [vm(a.shape if n[0] in "rl" else a.shape[1:]) for n, a in zip(NAMES, args)]
        more = scratch_of(r, cols, lq.shape[1], le.shape[1])
        scratch = staged + [vm(s) for s in more.values()]
        scratch += [pltpu.SemaphoreType.DMA((n,)) for n in (len(LOADS), 2, SENDS, len(SLOTS))]
        scratch.append(pltpu.SemaphoreType.REGULAR)
        return pl.pallas_call(
            functools.partial(kernel, tuple(more)),
            out_shape=jax.ShapeDtypeStruct(rhs.shape, F32),
            in_specs=[pl.BlockSpec(memory_space=pl.ANY)] * len(NAMES),
            out_specs=pl.BlockSpec(memory_space=pl.ANY),
            scratch_shapes=scratch,
            compiler_params=pltpu.CompilerParams(
                collective_id=0, has_side_effects=True, vmem_limit_bytes=60 * 1024 * 1024
            ),
        )(*args)

    leaves, chips = P(("leaf", "panel"), None, None), P("leaf", None, None)
    return jax.shard_map(
        local,
        mesh=mesh,
        in_specs=(P(("leaf", "panel"), None),) + (leaves,) * 8 + (chips,) * 8,
        out_specs=P(("leaf", "panel"), None),
        check_vma=False,
    )
```

```python
import functools

import jax
import jax.numpy as jnp
from jax import lax
from jax.experimental import pallas as pl
from jax.experimental.pallas import tpu as pltpu
from jax.sharding import PartitionSpec as P

MESH = pl.DeviceIdType.MESH
F32 = jnp.float32
NAMES = (
    ("rhs",)
    + ("lq", "le", "lf", "lg")
    + ("mq", "me", "mf", "mg")
    + ("pq", "pe", "pf", "pg")
    + ("uq", "ue", "uf", "ug")
)
LOADS = (
    [(n, None) for n in NAMES[13:] + NAMES[9:13] + NAMES[5:9]]
    + [("rhs", None)]
    + [(n, leaf) for leaf in (0, 1) for n in NAMES[1:4]]
    + [("lg", 0), ("lg", 1)]
)
RING, LINE = 8, 4


def nn(a, b):
    return lax.dot_general(
        a, b, (((1,), (0,)), ((), ())), precision=lax.Precision.HIGH, preferred_element_type=F32
    )


def nt(a, b):
    return lax.dot_general(
        a, b, (((1,), (1,)), ((), ())), precision=lax.Precision.HIGH, preferred_element_type=F32
    )


def pairs(b0, b1, m):
    r = b0.shape[1]
    return nn(b0, m[:r]) + nn(b1, m[r:])


def node_operators(q, e, f, g, mt, rt, p):
    r = e.shape[0]
    q1, q2 = q[:, :r], q[:, r:]
    tt = nt(q1, e[...])
    mt[...] = q2 - nt(tt, f[...])
    rt[...] = nt(tt, q1)
    p[...] = q2 - nn(q1, g[...])


def scratch_of(r, cols, size, e_rows):
    block, half, full, wide = (cols, r), (2 * r, r), (2 * r, 2 * r), (cols, 2 * r)
    ops = {}
    for n in ("m", "p", "u"):
        ops |= {n + "mt": half, n + "rt": full, n + "p": half}
    return ops | {
        "yl": (2, cols, e_rows), "xp": (2, size, cols), "lp": (2, size, r),
        "bm": (2, *block), "bp": (2, *block), "zm": block, "wm": block, "wo": block,
        "z0": block, "c1": block, "sib": block, "u1": block, "bpair": wide, "ppair": half,
        "w2": block, "m1": (r, r), "rt1": half, "p1": (r, r), "rt2": half, "p2": (r, r),
        "zq": (2, *block),
        "zg": (RING, *block), "z1": (4, *block), "z2": (2, *block), "w2s": (2, *block),
        "m2": (2, *half), "m3": half, "v3": (4 * r, r), "rt3": full, "p3": half, "g3": (r, r),
        "x3": (LINE, *block), "y5": (LINE, *block), "v5": (4 * r, r), "t3": (4 * r, r),
        "m4": (2, *half), "m5": half, "rt4": half, "p4": (r, r), "rt5": half, "p5": (r, r),
        "tt": (4 * r, r),
        "e0": (r, r), "my": (2, *half), "rt6": half, "p6": (r, r), "k7": half,
        "k7s": (2, *half), "tts": (4 * r, r),
    }


SLOTS = (
    [("bp", i) for i in (0, 1)]
    + [("zg", i) for i in range(RING)]
    + [(n, i) for n in ("x3", "y5") for i in range(LINE)]
    + [(n, i) for n in ("m2", "m4", "my") for i in (0, 1)]
    + [(n, 0) for n in ("wm", "sib", "w2", "zq", "m1", "rt1", "p1", "rt2", "p2")]
    + [(n, 0) for n in ("m3", "rt3", "p3", "m5")]
    + [(n, 0) for n in ("rt4", "p4", "rt5", "p5", "tt", "e0", "rt6", "p6", "k7")]
)
SENDS = 80


def kernel(names, *refs):
    n_in = len(NAMES)
    hbm, out = dict(zip(NAMES, refs[:n_in])), refs[n_in]
    refs = refs[n_in + 1 :]
    v, refs = dict(zip(NAMES, refs[:n_in])), refs[n_in:]
    t, refs = dict(zip(names, refs)), refs[len(names) :]
    load_sem, out_sem, send_sem, recv_sem, go = refs
    c, core = lax.axis_index("leaf"), lax.axis_index("panel")
    z, x, y = c % RING, (c // RING) % LINE, c // (RING * LINE)
    both = jnp.logical_and
    on0, on1 = core == 0, core == 1
    head0, head1 = both(on0, z == 0), both(on1, z == 0)
    column = both(head1, x == 0)
    inner = both(on0, z > 0)
    ring = c - z
    at_x = lambda q: c - RING * x + RING * q
    at_y = lambda q: c - RING * LINE * y + RING * LINE * q
    others = lambda i: [(i + d) % LINE for d in (1, 3, 2)]

    barrier = pltpu.get_barrier_semaphore()
    expected = []

    def greet(when, *devices):
        @pl.when(when)
        def _():
            for device in devices:
                pl.semaphore_signal(barrier, inc=1, device_id=device, device_id_type=MESH)

        expected.append(jnp.where(when, len(devices), 0))

    pl.semaphore_signal(barrier, inc=1, device_id=(c, 1 - core), device_id_type=MESH)
    greet(on0, (c + 1 - 2 * (z % 2), 0))
    greet(z > 0, (ring, 0))
    greet(both(on1, z % 2 == 1), (c - 1, 0))
    greet(both(on0, z % 2 == 0), (c + 1, 1))
    greet(head0, *((c + d, panel) for d in range(1, RING) for panel in (0, 1)))
    greet(both(on1, z % 4 == 2), *((c + d, 0) for d in (-2, -1, 1)))
    for place, d in ((0, 2), (1, 1), (3, -1)):
        greet(both(on0, z % 4 == place), (c + d, 1))
    greet(head0, *((at_x(q), panel) for q in others(x) for panel in (0, 1)))
    greet(head0, *((at_y(q), 0) for q in others(y)))
    greet(head1, *((at_x(q), 0) for q in others(x)))
    greet(column, *((at_y(q), 1) for q in others(y)))

    loads = {}
    for i, (n, leaf) in enumerate(LOADS):
        src, dst = hbm[n], v[n]
        if leaf is not None:
            src, dst = src.at[leaf], dst.at[leaf]
        elif n != "rhs":
            src = src.at[0]
        loads[n, leaf] = pltpu.make_async_copy(src, dst, load_sem.at[i])
        if n[0] in "up":
            pl.when(on1 if n[0] == "u" else on0)(loads[n, leaf].start)
        else:
            loads[n, leaf].start()

    def loaded(*keys):
        for n in keys:
            loads[n if isinstance(n, tuple) else (n, None)].wait()

    pending = []

    def slot(name, index):
        ref = t[name] if name in ALONE else t[name].at[index]
        return ref, recv_sem.at[SLOTS.index((name, 0)) + index]

    def copy_to(sem, src, device, name, index=0):
        dst, arrival = slot(name, index)
        return pltpu.make_async_remote_copy(
            src_ref=src, dst_ref=dst, send_sem=send_sem.at[sem], recv_sem=arrival,
            device_id=device, device_id_type=MESH,
        )

    used = [0]

    def send(when, *messages):
        copies = []
        for message in messages:
            copies.append(copy_to(used[0], *message))
            used[0] += 1
        pending.append((when, copies))

        @pl.when(when)
        def _():
            for copy in copies:
                copy.start()

    def sent():
        for when, copies in pending:
            @pl.when(when)
            def _():
                for copy in copies:
                    copy.wait_send()

        pending.clear()

    def arrived(name, index=0):
        copy_to(0, slot(name, index)[0], (c, 1 - core), name, index).wait_recv()

    r = v["ue"].shape[0]
    size = v["lq"].shape[1]
    e_rows = size - r

    def operators(n):
        loaded(*(n + k for k in "qefg"))
        node_operators(*(v[n + k] for k in "qefg"), t[n + "mt"], t[n + "rt"], t[n + "p"])

    umt, urt, up = t["umt"], t["urt"], t["up"]
    urts = [urt.at[:, :r], urt.at[:, r:]]
    ups = [up.at[:r], up.at[r:]]
    pl.when(on1)(lambda: operators("u"))
    pl.semaphore_wait(barrier, 1 + sum(expected[1:], expected[0]))
    send(both(column, y == 0), (v["ue"], (at_y(2), 1), "e0"))
    send(
        both(on1, z % 2 == 1),
        (umt.at[:r], (c - 1, 0), "m1"),
        (umt.at[r:], (c, 0), "m1"),
    )
    send(both(on1, z % 4 == 2), (umt, (ring, 0), "m2", z // 4))
    send(both(on1, z == 4), (umt, (ring, 0), "m3"))
    send(
        both(head1, x % 2 == 1),
        *((umt, (at_x(q), 0), "m4", x // 2) for q in others(x) + [x]),
        *((urts[s], (at_x(x - 1 + s), 0), "rt4") for s in (0, 1)),
        *((ups[s], (at_x(x - 1 + s), 0), "p4") for s in (0, 1)),
    )
    send(
        both(head1, x == 2),
        *((umt, (at_x(q), 0), "m5") for q in others(x) + [x]),
        *((urts[q // 2], (at_x(q), 0), "rt5") for q in range(LINE)),
        *((ups[q // 2], (at_x(q), 0), "p5") for q in range(LINE)),
    )
    send(
        both(column, y % 2 == 1),
        *((umt, (at_y(q), 1), "my", y // 2) for q in others(y)),
        (urts[0], (at_y(y - 1), 1), "rt6"),
        (ups[0], (at_y(y - 1), 1), "p6"),
    )

    operators("m")
    pl.when(on0)(lambda: operators("p"))

    loaded("rhs")
    bm, yl, bp = t["bm"], t["yl"], t["bp"]
    for leaf in (0, 1):
        bt = v["rhs"][leaf * size : (leaf + 1) * size, :].T
        loaded(("lq", leaf))
        ct = nn(bt, v["lq"][leaf])
        loaded(("le", leaf), ("lf", leaf))
        yt = nt(ct[:, :e_rows], v["le"][leaf])
        yl[leaf] = yt
        bm[leaf] = ct[:, e_rows:] - nt(yt, v["lf"][leaf])
    t["zm"][...] = pairs(bm[0], bm[1], t["mmt"])
    send(on1, (t["zm"], (c, 0), "bp", 1))

    @pl.when(both(column, y == 2))
    def _():
        arrived("e0")
        w7 = nt(umt[...], t["e0"][...])
        for s in (0, 1):
            t["k7s"][s] = urts[s][...] + nt(w7, ups[s][...])
        t["k7"][...] = t["k7s"][1]

    send(
        both(column, y == 2),
        *((t["k7s"].at[q // 2], (at_y(q), 1), "k7") for q in (1, 3, 0)),
    )
    for a in (0, 1):
        @pl.when(both(column, y == 2 * a + 1))
        def _():
            t["my"][a] = umt[...]
            t["rt6"][...] = urts[1][...]
            t["p6"][...] = ups[1][...]

        pl.when(both(column, y != 2 * a + 1))(lambda: arrived("my", a))

    @pl.when(both(column, y % 2 == 0))
    def _():
        arrived("rt6")
        arrived("p6")

    pl.when(both(column, y != 2))(lambda: arrived("k7"))

    @pl.when(column)
    def _():
        p6 = t["p6"][...]
        for a in (0, 1):
            rows = slice(2 * a * r, 2 * (a + 1) * r)
            own = jnp.where(y // 2 == a, t["rt6"][...], 0.0)
            t["tts"][rows] = nt(nn(t["my"][a], t["k7"][a * r : (a + 1) * r]), p6) + own

    send(column, *((t["tts"], (at_x(q), 0), "tt") for q in (1, 3, 2, 0)))

    zg, x3, y5 = t["zg"], t["x3"], t["y5"]

    @pl.when(on0)
    def _():
        bp[0] = t["zm"][...]
        arrived("bp", 1)
        z0 = pairs(bp[0], bp[1], t["pmt"])
        t["z0"][...] = z0
        arrived("m1")
        zg[0] = nn(z0, t["m1"][...])
        t["c1"][...] = zg[0]

    send(inner, (t["c1"], (ring, 0), "zg", z))
    send(on0, (t["z0"], (c + 1 - 2 * (z % 2), 0), "sib"))

    def leaf_parts():
        um = pairs(bm[0], bm[1], t["mrt"])
        for leaf in (0, 1):
            loaded(("lg", leaf))
            q1 = v["lq"][leaf, :, :e_rows]
            part = v["lq"][leaf, :, e_rows:] - nn(q1, v["lg"][leaf])
            t["xp"][leaf] = nt(q1, yl[leaf]) + nt(part, um[:, leaf * r : (leaf + 1) * r])
            t["lp"][leaf] = nn(part, t["mp"][leaf * r : (leaf + 1) * r])

    pl.when(on1)(leaf_parts)

    pl.when(both(on1, z > 0))(lambda: pl.semaphore_wait(go, 1))
    send(both(on1, z == 4), (up, (ring, 0), "p3"), (urt, (ring, 0), "rt3"))
    send(
        both(on1, z % 4 == 2),
        *((ups[m // 2], (c - 2 + m, 0), "p2") for m in range(4)),
        *((urts[m // 2], (c - 2 + m, 0), "rt2") for m in range(4)),
    )
    send(
        both(on1, z % 2 == 1),
        *((ups[s], (c - 1 + s, 0), "p1") for s in (0, 1)),
        *((urts[s], (c - 1 + s, 0), "rt1") for s in (0, 1)),
    )

    def chip_parts():
        for n in ("rt1", "p1", "rt2", "p2", "sib"):
            arrived(n)
        pl.when(z > 0)(lambda: arrived("zq"))
        p1, pp = t["p1"][...], t["pp"][...]
        first = jnp.where(z % 2 == 0, t["z0"][...], t["sib"][...])
        second = jnp.where(z % 2 == 0, t["sib"][...], t["z0"][...])
        u2 = pairs(t["zq"][0], t["zq"][1], t["rt2"])
        u1 = pairs(first, second, t["rt1"]) + nt(u2, p1)
        t["bpair"][...] = pairs(bp[0], bp[1], t["prt"]) + nt(u1, pp)
        t["ppair"][...] = nn(nn(pp, p1), t["p2"][...])

    @pl.when(head0)
    def _():
        for j in (0, 1):
            arrived("m2", j)
        arrived("m3")
        for i in (0, 1):
            rows = slice(2 * i * r, 2 * (i + 1) * r)
            t["v3"][rows] = nn(t["m2"][i], t["m3"][i * r : (i + 1) * r])
        z3 = 0.0
        for j in (0, 3, 1, 2):
            for i in (2 * j, 2 * j + 1):
                if i:
                    arrived("zg", i)
            if j == 0:
                pl.semaphore_signal(go, inc=1, device_id=(c + 4, 1), device_id_type=MESH)
            z1 = zg[2 * j] + zg[2 * j + 1]
            t["z1"][j] = z1
            z3 = z3 + nn(z1, t["v3"][j * r : (j + 1) * r])
        x3[x] = z3

    send(head0, *((x3.at[x], (at_x((x + d) % LINE), 0), "x3", x) for d in (2, 1, 3)))
    send(
        head0,
        *((t["z1"].at[i // 4 * 2 : i // 4 * 2 + 2], (c + i, 0), "zq") for i in (4, 5, 3, 6, 2, 7, 1)),
    )

    @pl.when(head0)
    def _():
        for i in (2, 6, 1, 3, 5, 7):
            pl.semaphore_signal(go, inc=1, device_id=(c + i, 1), device_id_type=MESH)
        for a in (0, 1):
            arrived("m4", a)
        for n in ("m5", "rt5", "p5", "rt4", "p4"):
            arrived(n)
        p4 = t["p4"][...]
        for a in (0, 1):
            rows, half = slice(2 * a * r, 2 * (a + 1) * r), slice(a * r, (a + 1) * r)
            m4 = t["m4"][a]
            t["v5"][rows] = nn(m4, t["m5"][half])
            own = jnp.where(x // 2 == a, t["rt4"][...], 0.0)
            t["t3"][rows] = nt(nn(m4, t["rt5"][half]), p4) + own
        t["g3"][...] = nn(p4, t["p5"][...])
        t["zq"][...] = t["z1"][:2]
        for i in (0, 1):
            t["z2"][i] = pairs(t["z1"][2 * i], t["z1"][2 * i + 1], t["m2"].at[i])
        for q in others(x):
            arrived("x3", q)
        y5[y] = sum(nn(x3[q], t["v5"][q * r : (q + 1) * r]) for q in range(LINE))

    send(head0, *((y5.at[y], (at_y((y + d) % LINE), 0), "y5", y) for d in (2, 1, 3)))

    @pl.when(head0)
    def _():
        b3 = sum(nn(x3[q], t["t3"][q * r : (q + 1) * r]) for q in range(LINE))
        arrived("p3")
        g2 = nn(t["p3"][...], t["g3"][...])
        arrived("rt3")
        b2 = pairs(t["z2"][0], t["z2"][1], t["rt3"]) + nt(b3, t["p3"][...])
        arrived("tt")
        for q in others(y):
            arrived("y5", q)
        w5 = sum(nn(y5[q], t["tt"][q * r : (q + 1) * r]) for q in range(LINE))
        w2 = b2 + nt(w5, g2)
        for i in (0, 1):
            t["w2s"][i] = w2[:, i * r : (i + 1) * r]
        t["w2"][...] = w2[:, :r]

    send(
        head0,
        *((t["w2s"].at[i // 4], (c + i, 0), "w2") for i in (4, 5, 3, 6, 2, 7, 1)),
    )
    late = pending.pop()
    sent()

    @pl.when(on0)
    def _():
        leaf_parts()
        chip_parts()
        pl.when(z > 0)(lambda: arrived("w2"))
        w = t["bpair"][...] + nt(t["w2"][...], t["ppair"][...])
        t["wo"][...] = w[:, r:]
        t["wm"][...] = w[:, :r]

    send(on0, (t["wo"], (c, 1), "wm"))
    pl.when(on1)(lambda: arrived("wm"))
    wm = t["wm"][...]
    outs = []
    for leaf in (0, 1):
        rows = slice(leaf * size, (leaf + 1) * size)
        v["rhs"][rows, :] = t["xp"][leaf] + nt(t["lp"][leaf], wm)
        outs.append(pltpu.make_async_copy(v["rhs"].at[rows], out.at[rows], out_sem.at[leaf]))
        outs[-1].start()
    for copy in outs:
        copy.wait()
    pending.append(late)
    sent()


ALONE = frozenset(n for n, _ in SLOTS if (n, 1) not in SLOTS)


def solution(mesh):
    def local(*args):
        rhs, lq, le = args[:3]
        r, cols = args[14].shape[1], rhs.shape[1]
        vm = lambda s: pltpu.VMEM(s, F32)
        staged = [vm(a.shape if n[0] in "rl" else a.shape[1:]) for n, a in zip(NAMES, args)]
        more = scratch_of(r, cols, lq.shape[1], le.shape[1])
        scratch = staged + [vm(s) for s in more.values()]
        scratch += [pltpu.SemaphoreType.DMA((n,)) for n in (len(LOADS), 2, SENDS, len(SLOTS))]
        scratch.append(pltpu.SemaphoreType.REGULAR)
        return pl.pallas_call(
            functools.partial(kernel, tuple(more)),
            out_shape=jax.ShapeDtypeStruct(rhs.shape, F32),
            in_specs=[pl.BlockSpec(memory_space=pl.ANY)] * len(NAMES),
            out_specs=pl.BlockSpec(memory_space=pl.ANY),
            scratch_shapes=scratch,
            compiler_params=pltpu.CompilerParams(
                collective_id=0, has_side_effects=True, vmem_limit_bytes=60 * 1024 * 1024
            ),
        )(*args)

    leaves, chips = P(("leaf", "panel"), None, None), P("leaf", None, None)
    return jax.shard_map(
        local,
        mesh=mesh,
        in_specs=(P(("leaf", "panel"), None),) + (leaves,) * 8 + (chips,) * 8,
        out_specs=P(("leaf", "panel"), None),
        check_vma=False,
    )
```

```python
import functools

import jax
import jax.numpy as jnp
from jax import lax
from jax.experimental import pallas as pl
from jax.experimental.pallas import tpu as pltpu
from jax.sharding import PartitionSpec as P

MESH = pl.DeviceIdType.MESH
F32 = jnp.float32
NAMES = (
    ("rhs",)
    + ("lq", "le", "lf", "lg")
    + ("mq", "me", "mf", "mg")
    + ("pq", "pe", "pf", "pg")
    + ("uq", "ue", "uf", "ug")
)
LOADS = (
    [(n, None) for n in NAMES[13:] + NAMES[9:13] + NAMES[5:9]]
    + [("rhs", None)]
    + [(n, leaf) for leaf in (0, 1) for n in NAMES[1:4]]
    + [("lg", 0), ("lg", 1)]
)
RING, LINE = 8, 4


def nn(a, b):
    return lax.dot_general(
        a, b, (((1,), (0,)), ((), ())), precision=lax.Precision.HIGH, preferred_element_type=F32
    )


def nt(a, b):
    return lax.dot_general(
        a, b, (((1,), (1,)), ((), ())), precision=lax.Precision.HIGH, preferred_element_type=F32
    )


def pairs(b0, b1, m):
    r = b0.shape[1]
    return nn(b0, m[:r]) + nn(b1, m[r:])


def node_operators(q, e, f, g, mt, rt, p):
    r = e.shape[0]
    q1, q2 = q[:, :r], q[:, r:]
    tt = nt(q1, e[...])
    mt[...] = q2 - nt(tt, f[...])
    rt[...] = nt(tt, q1)
    p[...] = q2 - nn(q1, g[...])


def scratch_of(r, cols, size, e_rows):
    block, half, full, wide = (cols, r), (2 * r, r), (2 * r, 2 * r), (cols, 2 * r)
    ops = {}
    for n in ("m", "p", "u"):
        ops |= {n + "mt": half, n + "rt": full, n + "p": half}
    return ops | {
        "yl": (2, cols, e_rows), "xp": (2, size, cols), "lp": (2, size, r),
        "bm": (2, *block), "bp": (2, *block), "zm": block,
        "z0": block, "c1": block, "sib": block, "u1": block, "bpair": wide, "ppair": half,
        "w2": block, "m1": (r, r), "rt1": half, "p1": (r, r), "rt2": half, "p2": (r, r),
        "zq": (2, *block), "bq": block, "pq": (r, r), "pm": half,
        "zg": (RING, *block), "z1": (4, *block), "z2": (2, *block), "w2s": (2, *block),
        "m2": (2, *half), "m3": half, "v3": (4 * r, r), "rt3": full, "p3": half, "g3": (r, r),
        "x3": (LINE, *block), "y5": (LINE, *block), "v5": (4 * r, r), "t3": (4 * r, r),
        "m4": (2, *half), "m5": half, "rt4": half, "p4": (r, r), "rt5": half, "p5": (r, r),
        "tt": (4 * r, r),
        "e0": (r, r), "my": (2, *half), "rt6": half, "p6": (r, r), "k7": half,
        "k7s": (2, *half), "tts": (4 * r, r),
    }


SLOTS = (
    [("bp", i) for i in (0, 1)]
    + [("zg", i) for i in range(RING)]
    + [(n, i) for n in ("x3", "y5") for i in range(LINE)]
    + [(n, i) for n in ("m2", "m4", "my") for i in (0, 1)]
    + [(n, 0) for n in ("bq", "pq", "sib", "w2", "zq", "m1", "rt1", "p1", "rt2", "p2")]
    + [(n, 0) for n in ("m3", "rt3", "p3", "m5")]
    + [(n, 0) for n in ("rt4", "p4", "rt5", "p5", "tt", "e0", "rt6", "p6", "k7")]
)
SENDS = 80


def kernel(names, *refs):
    n_in = len(NAMES)
    hbm, out = dict(zip(NAMES, refs[:n_in])), refs[n_in]
    refs = refs[n_in + 1 :]
    v, refs = dict(zip(NAMES, refs[:n_in])), refs[n_in:]
    t, refs = dict(zip(names, refs)), refs[len(names) :]
    load_sem, out_sem, send_sem, recv_sem, go = refs
    c, core = lax.axis_index("leaf"), lax.axis_index("panel")
    z, x, y = c % RING, (c // RING) % LINE, c // (RING * LINE)
    both = jnp.logical_and
    on0, on1 = core == 0, core == 1
    head0, head1 = both(on0, z == 0), both(on1, z == 0)
    column = both(head1, x == 0)
    inner = both(on0, z > 0)
    ring = c - z
    at_x = lambda q: c - RING * x + RING * q
    at_y = lambda q: c - RING * LINE * y + RING * LINE * q
    others = lambda i: [(i + d) % LINE for d in (1, 3, 2)]

    barrier = pltpu.get_barrier_semaphore()
    expected = []

    def greet(when, *devices):
        @pl.when(when)
        def _():
            for device in devices:
                pl.semaphore_signal(barrier, inc=1, device_id=device, device_id_type=MESH)

        expected.append(jnp.where(when, len(devices), 0))

    pl.semaphore_signal(barrier, inc=1, device_id=(c, 1 - core), device_id_type=MESH)
    greet(on0, (c + 1 - 2 * (z % 2), 0))
    greet(z > 0, (ring, 0))
    greet(both(on1, z % 2 == 1), (c - 1, 0))
    greet(both(on0, z % 2 == 0), (c + 1, 1))
    greet(head0, *((c + d, panel) for d in range(1, RING) for panel in (0, 1)))
    greet(both(on1, z % 4 == 2), *((c + d, 0) for d in (-2, -1, 1)))
    for place, d in ((0, 2), (1, 1), (3, -1)):
        greet(both(on0, z % 4 == place), (c + d, 1))
    greet(head0, *((at_x(q), panel) for q in others(x) for panel in (0, 1)))
    greet(head0, *((at_y(q), 0) for q in others(y)))
    greet(head1, *((at_x(q), 0) for q in others(x)))
    greet(column, *((at_y(q), 1) for q in others(y)))

    loads = {}
    for i, (n, leaf) in enumerate(LOADS):
        src, dst = hbm[n], v[n]
        if leaf is not None:
            src, dst = src.at[leaf], dst.at[leaf]
        elif n != "rhs":
            src = src.at[0]
        loads[n, leaf] = pltpu.make_async_copy(src, dst, load_sem.at[i])
        if n[0] in "up":
            pl.when(on1 if n[0] == "u" else on0)(loads[n, leaf].start)
        else:
            loads[n, leaf].start()

    def loaded(*keys):
        for n in keys:
            loads[n if isinstance(n, tuple) else (n, None)].wait()

    pending = []

    def slot(name, index):
        ref = t[name] if name in ALONE else t[name].at[index]
        return ref, recv_sem.at[SLOTS.index((name, 0)) + index]

    def copy_to(sem, src, device, name, index=0):
        dst, arrival = slot(name, index)
        return pltpu.make_async_remote_copy(
            src_ref=src, dst_ref=dst, send_sem=send_sem.at[sem], recv_sem=arrival,
            device_id=device, device_id_type=MESH,
        )

    used = [0]

    def send(when, *messages):
        copies = []
        for message in messages:
            copies.append(copy_to(used[0], *message))
            used[0] += 1
        pending.append((when, copies))

        @pl.when(when)
        def _():
            for copy in copies:
                copy.start()

    def sent():
        for when, copies in pending:
            @pl.when(when)
            def _():
                for copy in copies:
                    copy.wait_send()

        pending.clear()

    def arrived(name, index=0):
        copy_to(0, slot(name, index)[0], (c, 1 - core), name, index).wait_recv()

    r = v["ue"].shape[0]
    size = v["lq"].shape[1]
    e_rows = size - r

    def operators(n):
        loaded(*(n + k for k in "qefg"))
        node_operators(*(v[n + k] for k in "qefg"), t[n + "mt"], t[n + "rt"], t[n + "p"])

    umt, urt, up = t["umt"], t["urt"], t["up"]
    urts = [urt.at[:, :r], urt.at[:, r:]]
    ups = [up.at[:r], up.at[r:]]
    pl.when(on1)(lambda: operators("u"))
    pl.semaphore_wait(barrier, 1 + sum(expected[1:], expected[0]))
    send(both(column, y == 0), (v["ue"], (at_y(2), 1), "e0"))
    send(
        both(on1, z % 2 == 1),
        (umt.at[:r], (c - 1, 0), "m1"),
        (umt.at[r:], (c, 0), "m1"),
    )
    send(both(on1, z % 4 == 2), (umt, (ring, 0), "m2", z // 4))
    send(both(on1, z == 4), (umt, (ring, 0), "m3"))
    send(
        both(head1, x % 2 == 1),
        *((umt, (at_x(q), 0), "m4", x // 2) for q in others(x) + [x]),
        *((urts[s], (at_x(x - 1 + s), 0), "rt4") for s in (0, 1)),
        *((ups[s], (at_x(x - 1 + s), 0), "p4") for s in (0, 1)),
    )
    send(
        both(head1, x == 2),
        *((umt, (at_x(q), 0), "m5") for q in others(x) + [x]),
        *((urts[q // 2], (at_x(q), 0), "rt5") for q in range(LINE)),
        *((ups[q // 2], (at_x(q), 0), "p5") for q in range(LINE)),
    )
    send(
        both(column, y % 2 == 1),
        *((umt, (at_y(q), 1), "my", y // 2) for q in others(y)),
        (urts[0], (at_y(y - 1), 1), "rt6"),
        (ups[0], (at_y(y - 1), 1), "p6"),
    )

    operators("m")
    pl.when(on0)(lambda: operators("p"))

    loaded("rhs")
    bm, yl, bp = t["bm"], t["yl"], t["bp"]
    for leaf in (0, 1):
        bt = v["rhs"][leaf * size : (leaf + 1) * size, :].T
        loaded(("lq", leaf))
        ct = nn(bt, v["lq"][leaf])
        loaded(("le", leaf), ("lf", leaf))
        yt = nt(ct[:, :e_rows], v["le"][leaf])
        yl[leaf] = yt
        bm[leaf] = ct[:, e_rows:] - nt(yt, v["lf"][leaf])
    t["zm"][...] = pairs(bm[0], bm[1], t["mmt"])
    send(on1, (t["zm"], (c, 0), "bp", 1))

    @pl.when(both(column, y == 2))
    def _():
        arrived("e0")
        w7 = nt(umt[...], t["e0"][...])
        for s in (0, 1):
            t["k7s"][s] = urts[s][...] + nt(w7, ups[s][...])
        t["k7"][...] = t["k7s"][1]

    send(
        both(column, y == 2),
        *((t["k7s"].at[q // 2], (at_y(q), 1), "k7") for q in (1, 3, 0)),
    )
    for a in (0, 1):
        @pl.when(both(column, y == 2 * a + 1))
        def _():
            t["my"][a] = umt[...]
            t["rt6"][...] = urts[1][...]
            t["p6"][...] = ups[1][...]

        pl.when(both(column, y != 2 * a + 1))(lambda: arrived("my", a))

    @pl.when(both(column, y % 2 == 0))
    def _():
        arrived("rt6")
        arrived("p6")

    pl.when(both(column, y != 2))(lambda: arrived("k7"))

    @pl.when(column)
    def _():
        p6 = t["p6"][...]
        for a in (0, 1):
            rows = slice(2 * a * r, 2 * (a + 1) * r)
            own = jnp.where(y // 2 == a, t["rt6"][...], 0.0)
            t["tts"][rows] = nt(nn(t["my"][a], t["k7"][a * r : (a + 1) * r]), p6) + own

    send(column, *((t["tts"], (at_x(q), 0), "tt") for q in (1, 3, 2, 0)))

    zg, x3, y5 = t["zg"], t["x3"], t["y5"]

    @pl.when(on0)
    def _():
        arrived("m1")
        t["pm"][...] = nn(t["pmt"][...], t["m1"][...])
        bp[0] = t["zm"][...]
        arrived("bp", 1)
        c1 = pairs(bp[0], bp[1], t["pm"])
        t["c1"][...] = c1
        zg[0] = c1

    send(inner, (t["c1"], (ring, 0), "zg", z))

    @pl.when(on0)
    def _():
        t["z0"][...] = pairs(bp[0], bp[1], t["pmt"])

    send(on0, (t["z0"], (c + 1 - 2 * (z % 2), 0), "sib"))

    def leaf_parts():
        um = pairs(bm[0], bm[1], t["mrt"])
        for leaf in (0, 1):
            loaded(("lg", leaf))
            q1 = v["lq"][leaf, :, :e_rows]
            part = v["lq"][leaf, :, e_rows:] - nn(q1, v["lg"][leaf])
            t["xp"][leaf] = nt(q1, yl[leaf]) + nt(part, um[:, leaf * r : (leaf + 1) * r])
            t["lp"][leaf] = nn(part, t["mp"][leaf * r : (leaf + 1) * r])

    pl.when(jnp.logical_or(on1, z == 0))(leaf_parts)

    pl.when(both(on1, z > 0))(lambda: pl.semaphore_wait(go, 1))
    send(both(on1, z == 4), (up, (ring, 0), "p3"), (urt, (ring, 0), "rt3"))
    send(
        both(on1, z % 4 == 2),
        *((ups[m // 2], (c - 2 + m, 0), "p2") for m in range(4)),
        *((urts[m // 2], (c - 2 + m, 0), "rt2") for m in range(4)),
    )
    send(
        both(on1, z % 2 == 1),
        *((ups[s], (c - 1 + s, 0), "p1") for s in (0, 1)),
        *((urts[s], (c - 1 + s, 0), "rt1") for s in (0, 1)),
    )

    def chip_parts():
        for n in ("rt1", "p1", "rt2", "p2", "sib"):
            arrived(n)
        pl.when(z > 0)(lambda: arrived("zq"))
        p1, pp = t["p1"][...], t["pp"][...]
        first = jnp.where(z % 2 == 0, t["z0"][...], t["sib"][...])
        second = jnp.where(z % 2 == 0, t["sib"][...], t["z0"][...])
        u2 = pairs(t["zq"][0], t["zq"][1], t["rt2"])
        u1 = pairs(first, second, t["rt1"]) + nt(u2, p1)
        t["bpair"][...] = pairs(bp[0], bp[1], t["prt"]) + nt(u1, pp)
        t["ppair"][...] = nn(nn(pp, p1), t["p2"][...])

    @pl.when(head0)
    def _():
        for j in (0, 1):
            arrived("m2", j)
        arrived("m3")
        for i in (0, 1):
            rows = slice(2 * i * r, 2 * (i + 1) * r)
            t["v3"][rows] = nn(t["m2"][i], t["m3"][i * r : (i + 1) * r])
        z3 = 0.0
        for j in (0, 3, 1, 2):
            for i in (2 * j, 2 * j + 1):
                if i:
                    arrived("zg", i)
            if j == 0:
                pl.semaphore_signal(go, inc=1, device_id=(c + 4, 1), device_id_type=MESH)
            z1 = zg[2 * j] + zg[2 * j + 1]
            t["z1"][j] = z1
            z3 = z3 + nn(z1, t["v3"][j * r : (j + 1) * r])
        x3[x] = z3

    send(head0, *((x3.at[x], (at_x((x + d) % LINE), 0), "x3", x) for d in (2, 1, 3)))
    send(
        head0,
        *((t["z1"].at[i // 4 * 2 : i // 4 * 2 + 2], (c + i, 0), "zq") for i in (4, 5, 3, 6, 2, 7, 1)),
    )

    @pl.when(head0)
    def _():
        for i in (2, 6, 1, 3, 5, 7):
            pl.semaphore_signal(go, inc=1, device_id=(c + i, 1), device_id_type=MESH)
        for a in (0, 1):
            arrived("m4", a)
        for n in ("m5", "rt5", "p5", "rt4", "p4"):
            arrived(n)
        p4 = t["p4"][...]
        for a in (0, 1):
            rows, half = slice(2 * a * r, 2 * (a + 1) * r), slice(a * r, (a + 1) * r)
            m4 = t["m4"][a]
            t["v5"][rows] = nn(m4, t["m5"][half])
            own = jnp.where(x // 2 == a, t["rt4"][...], 0.0)
            t["t3"][rows] = nt(nn(m4, t["rt5"][half]), p4) + own
        t["g3"][...] = nn(p4, t["p5"][...])
        t["zq"][...] = t["z1"][:2]
        for i in (0, 1):
            t["z2"][i] = pairs(t["z1"][2 * i], t["z1"][2 * i + 1], t["m2"].at[i])
        for q in others(x):
            arrived("x3", q)
        y5[y] = sum(nn(x3[q], t["v5"][q * r : (q + 1) * r]) for q in range(LINE))

    send(head0, *((y5.at[y], (at_y((y + d) % LINE), 0), "y5", y) for d in (2, 1, 3)))

    @pl.when(head0)
    def _():
        b3 = sum(nn(x3[q], t["t3"][q * r : (q + 1) * r]) for q in range(LINE))
        arrived("p3")
        g2 = nn(t["p3"][...], t["g3"][...])
        arrived("rt3")
        b2 = pairs(t["z2"][0], t["z2"][1], t["rt3"]) + nt(b3, t["p3"][...])
        arrived("tt")
        for q in others(y):
            arrived("y5", q)
        w5 = sum(nn(y5[q], t["tt"][q * r : (q + 1) * r]) for q in range(LINE))
        w2 = b2 + nt(w5, g2)
        for i in (0, 1):
            t["w2s"][i] = w2[:, i * r : (i + 1) * r]
        t["w2"][...] = w2[:, :r]

    send(
        head0,
        *((t["w2s"].at[i // 4], (c + i, 0), "w2") for i in (4, 5, 3, 6, 2, 7, 1)),
    )
    late = pending.pop()
    sent()

    @pl.when(on0)
    def _():
        pl.when(z > 0)(leaf_parts)
        chip_parts()
        t["bq"][...] = t["bpair"][:, :r]
        t["pq"][...] = t["ppair"][:r]

    send(
        on0,
        (t["ppair"].at[r:], (c, 1), "pq"),
        (t["bpair"].at[:, r:], (c, 1), "bq"),
    )

    @pl.when(on1)
    def _():
        arrived("pq")
        arrived("bq")

    for leaf in (0, 1):
        part = t["lp"][leaf]
        t["xp"][leaf] = t["xp"][leaf] + nt(part, t["bq"][...])
        t["lp"][leaf] = nn(part, t["pq"][...])
    pl.when(jnp.logical_or(on1, z > 0))(lambda: arrived("w2"))
    send(on0, (t["w2"], (c, 1), "w2"))
    w2 = t["w2"][...]
    for leaf in (0, 1):
        rows = slice(leaf * size, (leaf + 1) * size)
        out[rows, :] = t["xp"][leaf] + nt(t["lp"][leaf], w2)
    pending.append(late)
    sent()


ALONE = frozenset(n for n, _ in SLOTS if (n, 1) not in SLOTS)


def solution(mesh):
    def local(*args):
        rhs, lq, le = args[:3]
        r, cols = args[14].shape[1], rhs.shape[1]
        vm = lambda s: pltpu.VMEM(s, F32)
        staged = [vm(a.shape if n[0] in "rl" else a.shape[1:]) for n, a in zip(NAMES, args)]
        more = scratch_of(r, cols, lq.shape[1], le.shape[1])
        scratch = staged + [vm(s) for s in more.values()]
        scratch += [pltpu.SemaphoreType.DMA((n,)) for n in (len(LOADS), 2, SENDS, len(SLOTS))]
        scratch.append(pltpu.SemaphoreType.REGULAR)
        return pl.pallas_call(
            functools.partial(kernel, tuple(more)),
            out_shape=pltpu.VMEM(rhs.shape, F32),
            in_specs=[pl.BlockSpec(memory_space=pltpu.HBM)] * len(NAMES),
            out_specs=pl.BlockSpec(memory_space=pltpu.VMEM),
            scratch_shapes=scratch,
            compiler_params=pltpu.CompilerParams(
                collective_id=0, has_side_effects=True, vmem_limit_bytes=40 << 20
            ),
        )(*(pltpu.with_memory_space_constraint(a, pltpu.HBM) for a in args))

    leaves, chips = P(("leaf", "panel"), None, None), P("leaf", None, None)
    return jax.shard_map(
        local,
        mesh=mesh,
        in_specs=(P(("leaf", "panel"), None),) + (leaves,) * 8 + (chips,) * 8,
        out_specs=P(("leaf", "panel"), None),
        check_vma=False,
    )
```

```python
import functools

import jax
import jax.numpy as jnp
from jax import lax
from jax.experimental import pallas as pl
from jax.experimental.pallas import tpu as pltpu
from jax.sharding import PartitionSpec as P

MESH = pl.DeviceIdType.MESH
F32 = jnp.float32
NAMES = (
    ("rhs",)
    + ("lq", "le", "lf", "lg")
    + ("mq", "me", "mf", "mg")
    + ("pq", "pe", "pf", "pg")
    + ("uq", "ue", "uf", "ug")
)
LOADS = (
    [(n, None) for n in NAMES[13:] + NAMES[9:13] + NAMES[5:9]]
    + [("rhs", None)]
    + [(n, leaf) for leaf in (0, 1) for n in NAMES[1:4]]
    + [("lg", 0), ("lg", 1)]
)
RING, LINE = 8, 4


def nn(a, b):
    return lax.dot_general(
        a, b, (((1,), (0,)), ((), ())), precision=lax.Precision.HIGH, preferred_element_type=F32
    )


def nt(a, b):
    return lax.dot_general(
        a, b, (((1,), (1,)), ((), ())), precision=lax.Precision.HIGH, preferred_element_type=F32
    )


def pairs(b0, b1, m):
    r = b0.shape[1]
    return nn(b0, m[:r]) + nn(b1, m[r:])


def node_operators(q, e, f, g, mt, rt, p):
    r = e.shape[0]
    q1, q2 = q[:, :r], q[:, r:]
    tt = nt(q1, e[...])
    mt[...] = q2 - nt(tt, f[...])
    rt[...] = nt(tt, q1)
    p[...] = q2 - nn(q1, g[...])


def scratch_of(r, cols, size, e_rows):
    block, half, full, wide = (cols, r), (2 * r, r), (2 * r, 2 * r), (cols, 2 * r)
    ops = {}
    for n in ("m", "p", "u"):
        ops |= {n + "mt": half, n + "rt": full, n + "p": half}
    return ops | {
        "yl": (2, cols, e_rows), "xp": (2, size, cols), "lp": (2, size, r),
        "bm": (2, *block), "bp": (2, *block), "zm": block,
        "z0": block, "c1": block, "sib": block, "u1": block, "bpair": wide, "ppair": half,
        "w2": block, "m1": (r, r), "rt1": half, "p1": (r, r), "rt2": half, "p2": (r, r),
        "zq": (2, *block), "bq": block, "pq": (r, r), "pm": half,
        "zg": (RING, *block), "z1": (4, *block), "z2": (2, *block), "w2s": (2, *block),
        "m2": (2, *half), "m3": half, "v3": (4 * r, r), "rt3": full, "p3": half, "g3": (r, r),
        "x3": (LINE, *block), "y5": (LINE, *block), "v5": (4 * r, r), "t3": (4 * r, r),
        "m4": (2, *half), "m5": half, "rt4": half, "p4": (r, r), "rt5": half, "p5": (r, r),
        "tt": (4 * r, r), "tg": (4 * r, 2 * r),
        "e0": (r, r), "my": (2, *half), "rt6": half, "p6": (r, r), "k7": half,
        "k7s": (2, *half), "tts": (4 * r, r),
    }


SLOTS = (
    [("bp", i) for i in (0, 1)]
    + [("zg", i) for i in range(RING)]
    + [(n, i) for n in ("x3", "y5") for i in range(LINE)]
    + [(n, i) for n in ("m2", "m4", "my") for i in (0, 1)]
    + [(n, 0) for n in ("bq", "pq", "sib", "w2", "zq", "m1", "rt1", "p1", "rt2", "p2")]
    + [(n, 0) for n in ("m3", "rt3", "p3", "m5")]
    + [(n, 0) for n in ("rt4", "p4", "rt5", "p5", "tt", "e0", "rt6", "p6", "k7")]
)
SENDS = 80


def kernel(names, *refs):
    n_in = len(NAMES)
    hbm, out = dict(zip(NAMES, refs[:n_in])), refs[n_in]
    refs = refs[n_in + 1 :]
    v, refs = dict(zip(NAMES, refs[:n_in])), refs[n_in:]
    t, refs = dict(zip(names, refs)), refs[len(names) :]
    load_sem, out_sem, send_sem, recv_sem, go = refs
    c, core = lax.axis_index("leaf"), lax.axis_index("panel")
    z, x, y = c % RING, (c // RING) % LINE, c // (RING * LINE)
    both = jnp.logical_and
    on0, on1 = core == 0, core == 1
    head0, head1 = both(on0, z == 0), both(on1, z == 0)
    column = both(head1, x == 0)
    inner = both(on0, z > 0)
    ring = c - z
    at_x = lambda q: c - RING * x + RING * q
    at_y = lambda q: c - RING * LINE * y + RING * LINE * q
    others = lambda i: [(i + d) % LINE for d in (1, 3, 2)]

    barrier = pltpu.get_barrier_semaphore()
    expected = []

    def greet(when, *devices):
        @pl.when(when)
        def _():
            for device in devices:
                pl.semaphore_signal(barrier, inc=1, device_id=device, device_id_type=MESH)

        expected.append(jnp.where(when, len(devices), 0))

    pl.semaphore_signal(barrier, inc=1, device_id=(c, 1 - core), device_id_type=MESH)
    greet(on0, (c + 1 - 2 * (z % 2), 0))
    greet(z > 0, (ring, 0))
    greet(both(on1, z % 2 == 1), (c - 1, 0))
    greet(both(on0, z % 2 == 0), (c + 1, 1))
    greet(head0, *((c + d, panel) for d in range(1, RING) for panel in (0, 1)))
    greet(both(on1, z % 4 == 2), *((c + d, 0) for d in (-2, -1, 1)))
    for place, d in ((0, 2), (1, 1), (3, -1)):
        greet(both(on0, z % 4 == place), (c + d, 1))
    greet(head0, *((at_x(q), panel) for q in others(x) for panel in (0, 1)))
    greet(head0, *((at_y(q), 0) for q in others(y)))
    greet(head1, *((at_x(q), 0) for q in others(x)))
    greet(column, *((at_y(q), 1) for q in others(y)))

    loads = {}
    for i, (n, leaf) in enumerate(LOADS):
        src, dst = hbm[n], v[n]
        if leaf is not None:
            src, dst = src.at[leaf], dst.at[leaf]
        elif n != "rhs":
            src = src.at[0]
        loads[n, leaf] = pltpu.make_async_copy(src, dst, load_sem.at[i])
        if n[0] in "up":
            pl.when(on1 if n[0] == "u" else on0)(loads[n, leaf].start)
        else:
            loads[n, leaf].start()

    def loaded(*keys):
        for n in keys:
            loads[n if isinstance(n, tuple) else (n, None)].wait()

    pending = []

    def slot(name, index):
        ref = t[name] if name in ALONE else t[name].at[index]
        return ref, recv_sem.at[SLOTS.index((name, 0)) + index]

    def copy_to(sem, src, device, name, index=0):
        dst, arrival = slot(name, index)
        return pltpu.make_async_remote_copy(
            src_ref=src, dst_ref=dst, send_sem=send_sem.at[sem], recv_sem=arrival,
            device_id=device, device_id_type=MESH,
        )

    used = [0]

    def gathered(name, here, m):
        total = 0.0
        for d in (0, 1, 3, 2):
            q = (here + d) % LINE
            if d:
                arrived(name, q)
            total = total + nn(t[name][q], m[pl.ds(pl.multiple_of(q * r, r), r)])
        return total

    def send(when, *messages):
        copies = []
        for message in messages:
            copies.append(copy_to(used[0], *message))
            used[0] += 1
        pending.append((when, copies))

        @pl.when(when)
        def _():
            for copy in copies:
                copy.start()

    def sent():
        for when, copies in pending:
            @pl.when(when)
            def _():
                for copy in copies:
                    copy.wait_send()

        pending.clear()

    def arrived(name, index=0):
        copy_to(0, slot(name, index)[0], (c, 1 - core), name, index).wait_recv()

    r = v["ue"].shape[0]
    size = v["lq"].shape[1]
    e_rows = size - r

    def operators(n):
        loaded(*(n + k for k in "qefg"))
        node_operators(*(v[n + k] for k in "qefg"), t[n + "mt"], t[n + "rt"], t[n + "p"])

    umt, urt, up = t["umt"], t["urt"], t["up"]
    urts = [urt.at[:, :r], urt.at[:, r:]]
    ups = [up.at[:r], up.at[r:]]
    pl.when(on1)(lambda: operators("u"))
    pl.semaphore_wait(barrier, 1 + sum(expected[1:], expected[0]))
    send(both(column, y == 0), (v["ue"], (at_y(2), 1), "e0"))
    send(
        both(on1, z % 2 == 1),
        (umt.at[:r], (c - 1, 0), "m1"),
        (umt.at[r:], (c, 0), "m1"),
    )
    send(both(on1, z % 4 == 2), (umt, (ring, 0), "m2", z // 4))
    send(both(on1, z == 4), (umt, (ring, 0), "m3"))
    send(
        both(head1, x % 2 == 1),
        *((umt, (at_x(q), 0), "m4", x // 2) for q in others(x) + [x]),
        *((urts[s], (at_x(x - 1 + s), 0), "rt4") for s in (0, 1)),
        *((ups[s], (at_x(x - 1 + s), 0), "p4") for s in (0, 1)),
    )
    send(
        both(head1, x == 2),
        *((umt, (at_x(q), 0), "m5") for q in others(x) + [x]),
        *((urts[q // 2], (at_x(q), 0), "rt5") for q in range(LINE)),
        *((ups[q // 2], (at_x(q), 0), "p5") for q in range(LINE)),
    )
    send(
        both(column, y % 2 == 1),
        *((umt, (at_y(q), 1), "my", y // 2) for q in others(y)),
        (urts[0], (at_y(y - 1), 1), "rt6"),
        (ups[0], (at_y(y - 1), 1), "p6"),
    )

    operators("m")
    pl.when(on0)(lambda: operators("p"))

    loaded("rhs")
    bm, yl, bp = t["bm"], t["yl"], t["bp"]
    loaded(*((n, leaf) for n in ("lq", "le", "lf") for leaf in (0, 1)))
    ct = [nn(v["rhs"][i * size : (i + 1) * size, :].T, v["lq"][i]) for i in (0, 1)]
    yt = [nt(ct[i][:, :e_rows], v["le"][i]) for i in (0, 1)]
    for leaf in (0, 1):
        yl[leaf] = yt[leaf]
        bm[leaf] = ct[leaf][:, e_rows:] - nt(yt[leaf], v["lf"][leaf])
    t["zm"][...] = pairs(bm[0], bm[1], t["mmt"])
    send(on1, (t["zm"], (c, 0), "bp", 1))

    @pl.when(both(column, y == 2))
    def _():
        arrived("e0")
        w7 = nt(umt[...], t["e0"][...])
        for s in (0, 1):
            t["k7s"][s] = urts[s][...] + nt(w7, ups[s][...])
        t["k7"][...] = t["k7s"][1]

    send(
        both(column, y == 2),
        *((t["k7s"].at[q // 2], (at_y(q), 1), "k7") for q in (1, 3, 0)),
    )
    for a in (0, 1):
        @pl.when(both(column, y == 2 * a + 1))
        def _():
            t["my"][a] = umt[...]
            t["rt6"][...] = urts[1][...]
            t["p6"][...] = ups[1][...]

        pl.when(both(column, y != 2 * a + 1))(lambda: arrived("my", a))

    @pl.when(both(column, y % 2 == 0))
    def _():
        arrived("rt6")
        arrived("p6")

    pl.when(both(column, y != 2))(lambda: arrived("k7"))

    @pl.when(column)
    def _():
        p6 = t["p6"][...]
        for a in (0, 1):
            rows = slice(2 * a * r, 2 * (a + 1) * r)
            own = jnp.where(y // 2 == a, t["rt6"][...], 0.0)
            t["tts"][rows] = nt(nn(t["my"][a], t["k7"][a * r : (a + 1) * r]), p6) + own

    send(column, *((t["tts"], (at_x(q), 0), "tt") for q in (1, 3, 2, 0)))

    zg, x3, y5 = t["zg"], t["x3"], t["y5"]

    @pl.when(on0)
    def _():
        arrived("m1")
        t["pm"][...] = nn(t["pmt"][...], t["m1"][...])
        bp[0] = t["zm"][...]
        c1 = nn(bp[0], t["pm"][:r])
        arrived("bp", 1)
        c1 = c1 + nn(bp[1], t["pm"][r:])
        t["c1"][...] = c1
        zg[0] = c1

    send(inner, (t["c1"], (ring, 0), "zg", z))

    @pl.when(on0)
    def _():
        t["z0"][...] = pairs(bp[0], bp[1], t["pmt"])

    send(on0, (t["z0"], (c + 1 - 2 * (z % 2), 0), "sib"))

    def leaf_parts():
        um = pairs(bm[0], bm[1], t["mrt"])
        for leaf in (0, 1):
            loaded(("lg", leaf))
            q1 = v["lq"][leaf, :, :e_rows]
            part = v["lq"][leaf, :, e_rows:] - nn(q1, v["lg"][leaf])
            t["xp"][leaf] = nt(q1, yl[leaf]) + nt(part, um[:, leaf * r : (leaf + 1) * r])
            t["lp"][leaf] = nn(part, t["mp"][leaf * r : (leaf + 1) * r])

    pl.when(jnp.logical_or(on1, z == 0))(leaf_parts)

    pl.when(both(on1, z > 0))(lambda: pl.semaphore_wait(go, 1))
    send(both(on1, z == 4), (up, (ring, 0), "p3"), (urt, (ring, 0), "rt3"))
    send(
        both(on1, z % 4 == 2),
        *((ups[m // 2], (c - 2 + m, 0), "p2") for m in range(4)),
        *((urts[m // 2], (c - 2 + m, 0), "rt2") for m in range(4)),
    )
    send(
        both(on1, z % 2 == 1),
        *((ups[s], (c - 1 + s, 0), "p1") for s in (0, 1)),
        *((urts[s], (c - 1 + s, 0), "rt1") for s in (0, 1)),
    )

    def chip_parts():
        for n in ("rt1", "p1", "rt2", "p2", "sib"):
            arrived(n)
        pl.when(z > 0)(lambda: arrived("zq"))
        p1, pp = t["p1"][...], t["pp"][...]
        first = jnp.where(z % 2 == 0, t["z0"][...], t["sib"][...])
        second = jnp.where(z % 2 == 0, t["sib"][...], t["z0"][...])
        u2 = pairs(t["zq"][0], t["zq"][1], t["rt2"])
        u1 = pairs(first, second, t["rt1"]) + nt(u2, p1)
        t["bpair"][...] = pairs(bp[0], bp[1], t["prt"]) + nt(u1, pp)
        t["ppair"][...] = nn(nn(pp, p1), t["p2"][...])

    @pl.when(head0)
    def _():
        for j in (0, 1):
            arrived("m2", j)
        arrived("m3")
        for i in (0, 1):
            rows = slice(2 * i * r, 2 * (i + 1) * r)
            t["v3"][rows] = nn(t["m2"][i], t["m3"][i * r : (i + 1) * r])
        z3 = 0.0
        for j in (0, 3, 1, 2):
            for i in (2 * j, 2 * j + 1):
                if i:
                    arrived("zg", i)
            if j == 0:
                pl.semaphore_signal(go, inc=1, device_id=(c + 4, 1), device_id_type=MESH)
            z1 = zg[2 * j] + zg[2 * j + 1]
            t["z1"][j] = z1
            z3 = z3 + nn(z1, t["v3"][j * r : (j + 1) * r])
        x3[x] = z3

    send(head0, *((x3.at[x], (at_x((x + d) % LINE), 0), "x3", x) for d in (2, 1, 3)))
    send(
        head0,
        *((t["z1"].at[i // 4 * 2 : i // 4 * 2 + 2], (c + i, 0), "zq") for i in (4, 5, 3, 6, 2, 7, 1)),
    )

    @pl.when(head0)
    def _():
        for i in (2, 6, 1, 3, 5, 7):
            pl.semaphore_signal(go, inc=1, device_id=(c + i, 1), device_id_type=MESH)
        for a in (0, 1):
            arrived("m4", a)
        for n in ("m5", "rt5", "p5", "rt4", "p4"):
            arrived(n)
        p4 = t["p4"][...]
        for a in (0, 1):
            rows, half = slice(2 * a * r, 2 * (a + 1) * r), slice(a * r, (a + 1) * r)
            m4 = t["m4"][a]
            t["v5"][rows] = nn(m4, t["m5"][half])
            own = jnp.where(x // 2 == a, t["rt4"][...], 0.0)
            t["t3"][rows] = nt(nn(m4, t["rt5"][half]), p4) + own
        t["g3"][...] = nn(p4, t["p5"][...])
        t["zq"][...] = t["z1"][:2]
        for i in (0, 1):
            t["z2"][i] = pairs(t["z1"][2 * i], t["z1"][2 * i + 1], t["m2"].at[i])
        y5[y] = gathered("x3", x, t["v5"])

    send(head0, *((y5.at[y], (at_y((y + d) % LINE), 0), "y5", y) for d in (2, 1, 3)))

    @pl.when(head0)
    def _():
        b3 = sum(nn(x3[q], t["t3"][q * r : (q + 1) * r]) for q in range(LINE))
        arrived("p3")
        g2 = nn(t["p3"][...], t["g3"][...])
        arrived("rt3")
        b2 = pairs(t["z2"][0], t["z2"][1], t["rt3"]) + nt(b3, t["p3"][...])
        arrived("tt")
        t["tg"][...] = nt(t["tt"][...], g2)
        w2 = b2 + gathered("y5", y, t["tg"])
        for i in (0, 1):
            t["w2s"][i] = w2[:, i * r : (i + 1) * r]
        t["w2"][...] = w2[:, :r]

    send(
        head0,
        *((t["w2s"].at[i // 4], (c + i, 0), "w2") for i in (4, 5, 3, 6, 2, 7, 1)),
    )
    late = pending.pop()
    sent()

    @pl.when(on0)
    def _():
        pl.when(z > 0)(leaf_parts)
        chip_parts()
        t["bq"][...] = t["bpair"][:, :r]
        t["pq"][...] = t["ppair"][:r]

    send(
        on0,
        (t["ppair"].at[r:], (c, 1), "pq"),
        (t["bpair"].at[:, r:], (c, 1), "bq"),
    )

    @pl.when(on1)
    def _():
        arrived("pq")
        arrived("bq")

    for leaf in (0, 1):
        part = t["lp"][leaf]
        t["xp"][leaf] = t["xp"][leaf] + nt(part, t["bq"][...])
        t["lp"][leaf] = nn(part, t["pq"][...])
    pl.when(jnp.logical_or(on1, z > 0))(lambda: arrived("w2"))
    send(on0, (t["w2"], (c, 1), "w2"))
    w2 = t["w2"][...]
    for leaf in (0, 1):
        rows = slice(leaf * size, (leaf + 1) * size)
        out[rows, :] = t["xp"][leaf] + nt(t["lp"][leaf], w2)
    pending.append(late)
    sent()


ALONE = frozenset(n for n, _ in SLOTS if (n, 1) not in SLOTS)


def solution(mesh):
    def local(*args):
        rhs, lq, le = args[:3]
        r, cols = args[14].shape[1], rhs.shape[1]
        vm = lambda s: pltpu.VMEM(s, F32)
        staged = [vm(a.shape if n[0] in "rl" else a.shape[1:]) for n, a in zip(NAMES, args)]
        more = scratch_of(r, cols, lq.shape[1], le.shape[1])
        scratch = staged + [vm(s) for s in more.values()]
        scratch += [pltpu.SemaphoreType.DMA((n,)) for n in (len(LOADS), 2, SENDS, len(SLOTS))]
        scratch.append(pltpu.SemaphoreType.REGULAR)
        return pl.pallas_call(
            functools.partial(kernel, tuple(more)),
            out_shape=pltpu.VMEM(rhs.shape, F32),
            in_specs=[pl.BlockSpec(memory_space=pltpu.HBM)] * len(NAMES),
            out_specs=pl.BlockSpec(memory_space=pltpu.VMEM),
            scratch_shapes=scratch,
            compiler_params=pltpu.CompilerParams(
                collective_id=0, has_side_effects=True, vmem_limit_bytes=40 << 20
            ),
        )(*(pltpu.with_memory_space_constraint(a, pltpu.HBM) for a in args))

    leaves, chips = P(("leaf", "panel"), None, None), P("leaf", None, None)
    return jax.shard_map(
        local,
        mesh=mesh,
        in_specs=(P(("leaf", "panel"), None),) + (leaves,) * 8 + (chips,) * 8,
        out_specs=P(("leaf", "panel"), None),
        check_vma=False,
    )
```

```python
import functools

import jax
import jax.numpy as jnp
from jax import lax
from jax.experimental import pallas as pl
from jax.experimental.pallas import tpu as pltpu
from jax.sharding import PartitionSpec as P

MESH = pl.DeviceIdType.MESH
F32 = jnp.float32
NAMES = (
    ("rhs",)
    + ("lq", "le", "lf", "lg")
    + ("mq", "me", "mf", "mg")
    + ("pq", "pe", "pf", "pg")
    + ("uq", "ue", "uf", "ug")
)
LOADS = (
    [(n, None) for n in NAMES[13:] + NAMES[9:13] + NAMES[5:9]]
    + [("rhs", None)]
    + [(n, leaf) for leaf in (0, 1) for n in NAMES[1:4]]
    + [("lg", 0), ("lg", 1)]
)
RING, LINE = 8, 4


def nn(a, b):
    return lax.dot_general(
        a, b, (((1,), (0,)), ((), ())), precision=lax.Precision.HIGH, preferred_element_type=F32
    )


def nt(a, b):
    return lax.dot_general(
        a, b, (((1,), (1,)), ((), ())), precision=lax.Precision.HIGH, preferred_element_type=F32
    )


def pairs(b0, b1, m):
    r = b0.shape[1]
    return nn(b0, m[:r]) + nn(b1, m[r:])


def node_operators(q, e, f, g, mt, rt, p):
    r = e.shape[0]
    q1, q2 = q[:, :r], q[:, r:]
    tt = nt(q1, e[...])
    mt[...] = q2 - nt(tt, f[...])
    rt[...] = nt(tt, q1)
    p[...] = q2 - nn(q1, g[...])


def scratch_of(r, cols, size, e_rows):
    block, half, full, wide = (cols, r), (2 * r, r), (2 * r, 2 * r), (cols, 2 * r)
    ops = {}
    for n in ("m", "p", "u"):
        ops |= {n + "mt": half, n + "rt": full, n + "p": half}
    return ops | {
        "yl": (2, cols, e_rows), "xp": (2, size, cols), "lp": (2, size, r),
        "bm": (2, *block), "bp": (2, *block), "zm": block,
        "z0": block, "c1": block, "sib": block, "u1": block, "bpair": wide, "ppair": half,
        "w2": block, "m1": (r, r), "rt1": half, "p1": (r, r), "rt2": half, "p2": (r, r),
        "zq": (2, *block), "bq": block, "pq": (r, r), "pm": half,
        "zg": (RING, *block), "z1": (4, *block), "z2": (2, *block), "w2s": (2, *block),
        "m2": (2, *half), "m3": half, "v3": (4 * r, r), "rt3": full, "p3": half, "g3": (r, r),
        "x3": (LINE, *block), "y5": (LINE, *block), "v5": (4 * r, r), "t3": (4 * r, r),
        "m4": (2, *half), "m5": half, "rt4": half, "p4": (r, r), "rt5": half, "p5": (r, r),
        "tt": (4 * r, r), "tg": (4 * r, 2 * r),
        "e0": (r, r), "my": (2, *half), "rt6": half, "p6": (r, r), "k7": half,
        "k7s": (2, *half), "tts": (4 * r, r),
    }


SLOTS = (
    [("bp", i) for i in (0, 1)]
    + [("zg", i) for i in range(RING)]
    + [(n, i) for n in ("x3", "y5") for i in range(LINE)]
    + [(n, i) for n in ("m2", "m4", "my") for i in (0, 1)]
    + [(n, 0) for n in ("bq", "pq", "sib", "w2", "zq", "m1", "rt1", "p1", "rt2", "p2")]
    + [(n, 0) for n in ("m3", "rt3", "p3", "m5")]
    + [(n, 0) for n in ("rt4", "p4", "rt5", "p5", "tt", "e0", "rt6", "p6", "k7")]
)
SENDS = 80


def kernel(names, *refs):
    n_in = len(NAMES)
    hbm, out = dict(zip(NAMES, refs[:n_in])), refs[n_in]
    refs = refs[n_in + 1 :]
    v, refs = dict(zip(NAMES, refs[:n_in])), refs[n_in:]
    t, refs = dict(zip(names, refs)), refs[len(names) :]
    load_sem, out_sem, send_sem, recv_sem, go = refs
    c, core = lax.axis_index("leaf"), lax.axis_index("panel")
    z, x, y = c % RING, (c // RING) % LINE, c // (RING * LINE)
    both = jnp.logical_and
    on0, on1 = core == 0, core == 1
    head0, head1 = both(on0, z == 0), both(on1, z == 0)
    column = both(head1, x == 0)
    inner = both(on0, z > 0)
    ring = c - z
    at_x = lambda q: c - RING * x + RING * q
    at_y = lambda q: c - RING * LINE * y + RING * LINE * q
    others = lambda i: [(i + d) % LINE for d in (1, 3, 2)]

    barrier = pltpu.get_barrier_semaphore()
    expected = []

    def greet(when, *devices):
        @pl.when(when)
        def _():
            for device in devices:
                pl.semaphore_signal(barrier, inc=1, device_id=device, device_id_type=MESH)

        expected.append(jnp.where(when, len(devices), 0))

    pl.semaphore_signal(barrier, inc=1, device_id=(c, 1 - core), device_id_type=MESH)
    greet(on0, (c + 1 - 2 * (z % 2), 0))
    greet(z > 0, (ring, 0))
    greet(both(on1, z % 2 == 1), (c - 1, 0))
    greet(both(on0, z % 2 == 0), (c + 1, 1))
    greet(head0, *((c + d, panel) for d in range(1, RING) for panel in (0, 1)))
    greet(both(on1, z % 4 == 2), *((c + d, 0) for d in (-2, -1, 1)))
    for place, d in ((0, 2), (1, 1), (3, -1)):
        greet(both(on0, z % 4 == place), (c + d, 1))
    greet(head0, *((at_x(q), panel) for q in others(x) for panel in (0, 1)))
    greet(head0, *((at_y(q), 0) for q in others(y)))
    greet(head1, *((at_x(q), 0) for q in others(x)))
    greet(column, *((at_y(q), 1) for q in others(y)))

    loads = {}
    for i, (n, leaf) in enumerate(LOADS):
        src, dst = hbm[n], v[n]
        if leaf is not None:
            src, dst = src.at[leaf], dst.at[leaf]
        elif n != "rhs":
            src = src.at[0]
        loads[n, leaf] = pltpu.make_async_copy(src, dst, load_sem.at[i])
        if n[0] in "up":
            pl.when(on1 if n[0] == "u" else on0)(loads[n, leaf].start)
        else:
            loads[n, leaf].start()

    def loaded(*keys):
        for n in keys:
            loads[n if isinstance(n, tuple) else (n, None)].wait()

    pending = []

    def slot(name, index):
        ref = t[name] if name in ALONE else t[name].at[index]
        return ref, recv_sem.at[SLOTS.index((name, 0)) + index]

    def copy_to(sem, src, device, name, index=0):
        dst, arrival = slot(name, index)
        return pltpu.make_async_remote_copy(
            src_ref=src, dst_ref=dst, send_sem=send_sem.at[sem], recv_sem=arrival,
            device_id=device, device_id_type=MESH,
        )

    used = [0]

    def gathered(name, here, m):
        total = 0.0
        for d in (0, 1, 3, 2):
            q = (here + d) % LINE
            if d:
                arrived(name, q)
            total = total + nn(t[name][q], m[pl.ds(pl.multiple_of(q * r, r), r)])
        return total

    def send(when, *messages):
        copies = []
        for message in messages:
            copies.append(copy_to(used[0], *message))
            used[0] += 1
        pending.append((when, copies))

        @pl.when(when)
        def _():
            for copy in copies:
                copy.start()

    def sent():
        for when, copies in pending:
            @pl.when(when)
            def _():
                for copy in copies:
                    copy.wait_send()

        pending.clear()

    def arrived(name, index=0):
        copy_to(0, slot(name, index)[0], (c, 1 - core), name, index).wait_recv()

    r = v["ue"].shape[0]
    size = v["lq"].shape[1]
    e_rows = size - r

    def operators(n):
        loaded(*(n + k for k in "qefg"))
        node_operators(*(v[n + k] for k in "qefg"), t[n + "mt"], t[n + "rt"], t[n + "p"])

    umt, urt, up = t["umt"], t["urt"], t["up"]
    urts = [urt.at[:, :r], urt.at[:, r:]]
    ups = [up.at[:r], up.at[r:]]
    pl.when(on1)(lambda: operators("u"))
    pl.semaphore_wait(barrier, 1 + sum(expected[1:], expected[0]))
    send(both(column, y == 0), (v["ue"], (at_y(2), 1), "e0"))
    send(
        both(on1, z % 2 == 1),
        (umt.at[:r], (c - 1, 0), "m1"),
        (umt.at[r:], (c, 0), "m1"),
    )
    send(both(on1, z % 4 == 2), (umt, (ring, 0), "m2", z // 4))
    send(both(on1, z == 4), (umt, (ring, 0), "m3"))
    send(
        both(head1, x % 2 == 1),
        *((umt, (at_x(q), 0), "m4", x // 2) for q in others(x) + [x]),
        *((urts[s], (at_x(x - 1 + s), 0), "rt4") for s in (0, 1)),
        *((ups[s], (at_x(x - 1 + s), 0), "p4") for s in (0, 1)),
    )
    send(
        both(head1, x == 2),
        *((umt, (at_x(q), 0), "m5") for q in others(x) + [x]),
        *((urts[q // 2], (at_x(q), 0), "rt5") for q in range(LINE)),
        *((ups[q // 2], (at_x(q), 0), "p5") for q in range(LINE)),
    )
    send(
        both(column, y % 2 == 1),
        *((umt, (at_y(q), 1), "my", y // 2) for q in others(y)),
        (urts[0], (at_y(y - 1), 1), "rt6"),
        (ups[0], (at_y(y - 1), 1), "p6"),
    )

    operators("m")
    pl.when(on0)(lambda: operators("p"))

    loaded("rhs")
    bm, yl, bp = t["bm"], t["yl"], t["bp"]
    loaded(*((n, leaf) for n in ("lq", "le", "lf") for leaf in (0, 1)))
    ct = [nn(v["rhs"][i * size : (i + 1) * size, :].T, v["lq"][i]) for i in (0, 1)]
    yt = [nt(ct[i][:, :e_rows], v["le"][i]) for i in (0, 1)]
    for leaf in (0, 1):
        yl[leaf] = yt[leaf]
        bm[leaf] = ct[leaf][:, e_rows:] - nt(yt[leaf], v["lf"][leaf])
    t["zm"][...] = pairs(bm[0], bm[1], t["mmt"])
    send(on1, (t["zm"], (c, 0), "bp", 1))

    @pl.when(both(column, y == 2))
    def _():
        arrived("e0")
        w7 = nt(umt[...], t["e0"][...])
        for s in (0, 1):
            t["k7s"][s] = urts[s][...] + nt(w7, ups[s][...])
        t["k7"][...] = t["k7s"][1]

    send(
        both(column, y == 2),
        *((t["k7s"].at[q // 2], (at_y(q), 1), "k7") for q in (1, 3, 0)),
    )
    for a in (0, 1):
        @pl.when(both(column, y == 2 * a + 1))
        def _():
            t["my"][a] = umt[...]
            t["rt6"][...] = urts[1][...]
            t["p6"][...] = ups[1][...]

        pl.when(both(column, y != 2 * a + 1))(lambda: arrived("my", a))

    @pl.when(both(column, y % 2 == 0))
    def _():
        arrived("rt6")
        arrived("p6")

    pl.when(both(column, y != 2))(lambda: arrived("k7"))

    @pl.when(column)
    def _():
        p6 = t["p6"][...]
        for a in (0, 1):
            rows = slice(2 * a * r, 2 * (a + 1) * r)
            own = jnp.where(y // 2 == a, t["rt6"][...], 0.0)
            t["tts"][rows] = nt(nn(t["my"][a], t["k7"][a * r : (a + 1) * r]), p6) + own

    send(column, *((t["tts"], (at_x(q), 0), "tt") for q in (1, 3, 2, 0)))

    zg, x3, y5 = t["zg"], t["x3"], t["y5"]

    @pl.when(on0)
    def _():
        arrived("m1")
        t["pm"][...] = nn(t["pmt"][...], t["m1"][...])
        bp[0] = t["zm"][...]
        c1 = nn(bp[0], t["pm"][:r])
        arrived("bp", 1)
        c1 = c1 + nn(bp[1], t["pm"][r:])
        t["c1"][...] = c1
        zg[0] = c1

    send(inner, (t["c1"], (ring, 0), "zg", z))

    @pl.when(on0)
    def _():
        t["z0"][...] = pairs(bp[0], bp[1], t["pmt"])

    send(head0, (t["z0"], (c + 1, 0), "sib"))

    def leaf_parts():
        um = pairs(bm[0], bm[1], t["mrt"])
        for leaf in (0, 1):
            loaded(("lg", leaf))
            q1 = v["lq"][leaf, :, :e_rows]
            part = v["lq"][leaf, :, e_rows:] - nn(q1, v["lg"][leaf])
            t["xp"][leaf] = nt(q1, yl[leaf]) + nt(part, um[:, leaf * r : (leaf + 1) * r])
            t["lp"][leaf] = nn(part, t["mp"][leaf * r : (leaf + 1) * r])

    pl.when(jnp.logical_or(on1, z == 0))(leaf_parts)

    pl.when(both(on1, z > 0))(lambda: pl.semaphore_wait(go, 1))
    send(both(on1, z == 4), (up, (ring, 0), "p3"), (urt, (ring, 0), "rt3"))
    send(
        both(on1, z % 4 == 2),
        *((ups[m // 2], (c - 2 + m, 0), "p2") for m in range(4)),
        *((urts[m // 2], (c - 2 + m, 0), "rt2") for m in range(4)),
    )
    send(
        both(on1, z % 2 == 1),
        *((ups[s], (c - 1 + s, 0), "p1") for s in (0, 1)),
        *((urts[s], (c - 1 + s, 0), "rt1") for s in (0, 1)),
    )

    def chip_parts():
        for n in ("rt1", "p1", "rt2", "p2", "sib"):
            arrived(n)
        pl.when(z > 0)(lambda: arrived("zq"))
        p1, pp = t["p1"][...], t["pp"][...]
        first = jnp.where(z % 2 == 0, t["z0"][...], t["sib"][...])
        second = jnp.where(z % 2 == 0, t["sib"][...], t["z0"][...])
        u2 = pairs(t["zq"][0], t["zq"][1], t["rt2"])
        u1 = pairs(first, second, t["rt1"]) + nt(u2, p1)
        t["bpair"][...] = pairs(bp[0], bp[1], t["prt"]) + nt(u1, pp)
        t["ppair"][...] = nn(nn(pp, p1), t["p2"][...])

    @pl.when(head0)
    def _():
        for j in (0, 1):
            arrived("m2", j)
        arrived("m3")
        for i in (0, 1):
            rows = slice(2 * i * r, 2 * (i + 1) * r)
            t["v3"][rows] = nn(t["m2"][i], t["m3"][i * r : (i + 1) * r])
        z3 = 0.0
        for j in (0, 3, 1, 2):
            for i in (2 * j, 2 * j + 1):
                if i:
                    arrived("zg", i)
            if j == 0:
                pl.semaphore_signal(go, inc=1, device_id=(c + 4, 1), device_id_type=MESH)
            z1 = zg[2 * j] + zg[2 * j + 1]
            t["z1"][j] = z1
            z3 = z3 + nn(z1, t["v3"][j * r : (j + 1) * r])
        x3[x] = z3

    send(head0, *((x3.at[x], (at_x((x + d) % LINE), 0), "x3", x) for d in (2, 1, 3)))
    send(
        head0,
        *((t["z1"].at[i // 4 * 2 : i // 4 * 2 + 2], (c + i, 0), "zq") for i in (4, 5, 3, 6, 2, 7, 1)),
    )

    @pl.when(head0)
    def _():
        for i in (2, 6, 1, 3, 5, 7):
            pl.semaphore_signal(go, inc=1, device_id=(c + i, 1), device_id_type=MESH)
        for a in (0, 1):
            arrived("m4", a)
        for n in ("m5", "rt5", "p5", "rt4", "p4"):
            arrived(n)
        p4 = t["p4"][...]
        for a in (0, 1):
            rows, half = slice(2 * a * r, 2 * (a + 1) * r), slice(a * r, (a + 1) * r)
            m4 = t["m4"][a]
            t["v5"][rows] = nn(m4, t["m5"][half])
            own = jnp.where(x // 2 == a, t["rt4"][...], 0.0)
            t["t3"][rows] = nt(nn(m4, t["rt5"][half]), p4) + own
        t["g3"][...] = nn(p4, t["p5"][...])
        t["zq"][...] = t["z1"][:2]
        for i in (0, 1):
            t["z2"][i] = pairs(t["z1"][2 * i], t["z1"][2 * i + 1], t["m2"].at[i])
        y5[y] = gathered("x3", x, t["v5"])

    send(head0, *((y5.at[y], (at_y((y + d) % LINE), 0), "y5", y) for d in (2, 1, 3)))

    @pl.when(head0)
    def _():
        b3 = sum(nn(x3[q], t["t3"][q * r : (q + 1) * r]) for q in range(LINE))
        arrived("p3")
        g2 = nn(t["p3"][...], t["g3"][...])
        arrived("rt3")
        b2 = pairs(t["z2"][0], t["z2"][1], t["rt3"]) + nt(b3, t["p3"][...])
        arrived("tt")
        t["tg"][...] = nt(t["tt"][...], g2)
        for q in (0, 1, 3):
            if q:
                arrived("y5", (y + q) % LINE)
            rows = pl.ds(pl.multiple_of((y + q) % LINE * r, r), r)
            b2 = b2 + nn(y5[(y + q) % LINE], t["tg"][rows])
        arrived("y5", (y + 2) % LINE)
        rows = pl.ds(pl.multiple_of((y + 2) % LINE * r, r), r)
        t["w2s"][0] = b2[:, :r]
        t["w2s"][1] = b2[:, r:] + nn(y5[(y + 2) % LINE], t["tg"][rows, r:])

    send(head0, *((t["w2s"].at[1], (c + i, 0), "w2") for i in (4, 5, 6, 7)))

    @pl.when(head0)
    def _():
        rows = pl.ds(pl.multiple_of((y + 2) % LINE * r, r), r)
        w2 = t["w2s"][0] + nn(y5[(y + 2) % LINE], t["tg"][rows, :r])
        t["w2s"][0] = w2
        t["w2"][...] = w2

    send(head0, *((t["w2s"].at[0], (c + i, 0), "w2") for i in (3, 2, 1)))
    late = [pending.pop(), pending.pop()]
    sent()

    pl.when(inner)(leaf_parts)
    send(inner, (t["z0"], (c + 1 - 2 * (z % 2), 0), "sib"))

    @pl.when(on0)
    def _():
        chip_parts()
        t["bq"][...] = t["bpair"][:, :r]
        t["pq"][...] = t["ppair"][:r]

    send(
        on0,
        (t["ppair"].at[r:], (c, 1), "pq"),
        (t["bpair"].at[:, r:], (c, 1), "bq"),
    )

    @pl.when(on1)
    def _():
        arrived("pq")
        arrived("bq")

    for leaf in (0, 1):
        part = t["lp"][leaf]
        t["xp"][leaf] = t["xp"][leaf] + nt(part, t["bq"][...])
        t["lp"][leaf] = nn(part, t["pq"][...])
    pl.when(jnp.logical_or(on1, z > 0))(lambda: arrived("w2"))
    send(on0, (t["w2"], (c, 1), "w2"))
    w2 = t["w2"][...]
    for leaf in (0, 1):
        rows = slice(leaf * size, (leaf + 1) * size)
        out[rows, :] = t["xp"][leaf] + nt(t["lp"][leaf], w2)
    pending.extend(late)
    sent()


ALONE = frozenset(n for n, _ in SLOTS if (n, 1) not in SLOTS)


def solution(mesh):
    def local(*args):
        rhs, lq, le = args[:3]
        r, cols = args[14].shape[1], rhs.shape[1]
        vm = lambda s: pltpu.VMEM(s, F32)
        staged = [vm(a.shape if n[0] in "rl" else a.shape[1:]) for n, a in zip(NAMES, args)]
        more = scratch_of(r, cols, lq.shape[1], le.shape[1])
        scratch = staged + [vm(s) for s in more.values()]
        scratch += [pltpu.SemaphoreType.DMA((n,)) for n in (len(LOADS), 2, SENDS, len(SLOTS))]
        scratch.append(pltpu.SemaphoreType.REGULAR)
        return pl.pallas_call(
            functools.partial(kernel, tuple(more)),
            out_shape=pltpu.VMEM(rhs.shape, F32),
            in_specs=[pl.BlockSpec(memory_space=pltpu.HBM)] * len(NAMES),
            out_specs=pl.BlockSpec(memory_space=pltpu.VMEM),
            scratch_shapes=scratch,
            compiler_params=pltpu.CompilerParams(
                collective_id=0, has_side_effects=True, vmem_limit_bytes=40 << 20
            ),
        )(*(pltpu.with_memory_space_constraint(a, pltpu.HBM) for a in args))

    leaves, chips = P(("leaf", "panel"), None, None), P("leaf", None, None)
    return jax.shard_map(
        local,
        mesh=mesh,
        in_specs=(P(("leaf", "panel"), None),) + (leaves,) * 8 + (chips,) * 8,
        out_specs=P(("leaf", "panel"), None),
        check_vma=False,
    )
```
